32 devices in a mesh: dp: 4 (over y, x), seq: 8 (over z, core).
Axes of the slice: x: 2, y: 2, z: 4, core: 2. Of those that a mesh axis runs over, the one named last changes fastest.
Arguments:
- hidden: bfloat16 [8192, 1024], P(('dp', 'seq')), may hold values from -6 to 6
- encoder: bfloat16 [4096, 1024], P(('dp', 'seq')), may hold values from -6 to 6
- piece_starts: int32 [4, 2], P('dp'), may hold values from 0 to 1792, as said below
- grad_out: bfloat16 [8192, 1024], P(('dp', 'seq')), may hold values from -6 to 6
- attn_in: float32 [6, 1024, 1024], P(None, 'seq'), may hold values from -0.1875 to 0.1875
- attn_out: float32 [2, 1024, 1024], P(None, 'seq'), may hold values from -4 to 4
- ffn_in: float32 [1024, 8192], P('seq'), may hold values from -0.1875 to 0.1875
- ffn_out: float32 [8192, 1024], P('seq'), may hold values from -0.0625 to 0.0625
- norms: float32 [6, 1024], replicated, may hold values from -0.2 to 1.5, as said below
- first_attn_in: float32 [6, 1024, 1024], P(None, 'seq'), may hold values from -0.036 to 0.036
- first_attn_out: float32 [2, 1024, 1024], P(None, 'seq'), may hold values from -0.036 to 0.036
- first_ffn_in: float32 [1024, 8192], P('seq'), may hold values from -0.036 to 0.036
- first_ffn_out: float32 [8192, 1024], P('seq'), may hold values from -0.036 to 0.036
- first_norms: float32 [6, 1024], replicated, may hold values from -0.036 to 0.036
- second_attn_in: float32 [6, 1024, 1024], P(None, 'seq'), may hold values from 1e-05 to 0.001
- second_attn_out: float32 [2, 1024, 1024], P(None, 'seq'), may hold values from 1e-05 to 0.001
- second_ffn_in: float32 [1024, 8192], P('seq'), may hold values from 1e-05 to 0.001
- second_ffn_out: float32 [8192, 1024], P('seq'), may hold values from 1e-05 to 0.001
- second_norms: float32 [6, 1024], replicated, may hold values from 1e-05 to 0.001
Outputs:
- out_hidden: float32 [8192, 1024], P(('dp', 'seq'))
- grad_hidden: float32 [8192, 1024], P(('dp', 'seq'))
- grad_encoder: float32 [4096, 1024], P(('dp', 'seq'))
- grad_attn_in: float32 [6, 1024, 1024], P(None, 'seq')
- grad_attn_out: float32 [2, 1024, 1024], P(None, 'seq')
- grad_ffn_in: float32 [1024, 8192], P('seq')
- grad_ffn_out: float32 [8192, 1024], P('seq')
- grad_norms: float32 [6, 1024], replicated
- new_first_attn_in: float32 [6, 1024, 1024], P(None, 'seq')
- new_first_attn_out: float32 [2, 1024, 1024], P(None, 'seq')
- new_first_ffn_in: float32 [1024, 8192], P('seq')
- new_first_ffn_out: float32 [8192, 1024], P('seq')
- new_first_norms: float32 [6, 1024], replicated
- new_second_attn_in: float32 [6, 1024, 1024], P(None, 'seq')
- new_second_attn_out: float32 [2, 1024, 1024], P(None, 'seq')
- new_second_ffn_in: float32 [1024, 8192], P('seq')
- new_second_ffn_out: float32 [8192, 1024], P('seq')
- new_second_norms: float32 [6, 1024], replicated
- change_attn_in: float32 [6, 1024, 1024], P(None, 'seq')
- change_attn_out: float32 [2, 1024, 1024], P(None, 'seq')
- change_ffn_in: float32 [1024, 8192], P('seq')
- change_ffn_out: float32 [8192, 1024], P('seq')
- change_norms: float32 [6, 1024], replicated
The draws below stay inside these ranges and needn't reach their ends.
Inputs may be any that keep to these rules, and one draw needn't show every extreme that they name: `piece_starts`: in each sequence the 2 starts rise, each piece of 256 tokens ends before the next one starts, and every piece lies inside the sequence. `norms`: rows 0, 2, 4 are gains, rows 1, 3, 5 biases.
All inputs are finite; a program needn't handle non-finite values.
Results may differ from the reference program's by a relative error of at most 0.025.
Values may be sent and summed in bfloat16 or wider, within the bound.
No kernel may reach another device: no remote copies, remote signals or barrier semaphores. Data moves between devices by JAX's collectives and lax.ppermute only.
A program may use at most 448 MiB of HBM per device.

```python
import math
import jax
import jax.numpy as jnp
from jax import lax

D = 1024
HEADS = 16
HEAD_DIM = 64
FF = 8192
ENC = 1024
PIECE_LEN = 256
SEQ_LEN = 2048
GROUPS = 4
TOKENS = 8192
PIECES = 2


def draw_piece_starts(key, part):
    windows = SEQ_LEN // (2 * PIECE_LEN)

    def one_sequence(sub_key):
        chosen = jnp.sort(jax.random.permutation(jax.random.fold_in(sub_key, 1), windows)[:PIECES])
        offset = jax.random.randint(jax.random.fold_in(sub_key, 2), (PIECES,), 0, PIECE_LEN + 1)
        return (chosen * 2 * PIECE_LEN + offset).astype(jnp.int32)
    return jax.vmap(one_sequence)(jax.random.split(jax.random.fold_in(key, 7), GROUPS))


def draw_norms(key, part):
    unit = jax.random.uniform(jax.random.fold_in(key, 11), (6, D), dtype=jnp.float32)
    row_index = lax.broadcasted_iota(jnp.int32, (6, D), 0)
    return jnp.where(row_index % 2 == 0, 0.5 + unit, 0.4 * unit - 0.2)


def level_of(stream_key, dims, pieces, smallest, high):
    level, own = 1.0, jax.random.fold_in(stream_key, 6)
    for axis_at, parts in pieces:
        draws = jnp.exp(jax.random.uniform(jax.random.fold_in(own, axis_at), (parts,), jnp.float32, smallest / len(pieces), high / len(pieces)))
        level = level * jnp.repeat(draws, dims[axis_at] // parts).reshape([-1 if axis == axis_at else 1 for axis in range(len(dims))])
    return level


def gaussian(key, dims, spread, limit, shards=(), kind=jnp.bfloat16):
    loudness = level_of(key, dims, shards, -0.22, 0.18) if shards else 1.0
    drawn = jax.random.normal(key, dims, jnp.float32) * spread * loudness
    return jnp.minimum(jnp.maximum(drawn, -limit), limit).astype(kind)


def setup_inputs(seed: int = 0) -> dict:
    key_list = jax.random.split(jax.random.key(seed), 20)
    hidden = gaussian(key_list[0], (TOKENS, D), 1.0, 6.0, ((0, 32),))
    encoder = gaussian(key_list[1], (GROUPS * ENC, D), 1.0, 6.0, ((0, 32),))
    piece_starts = draw_piece_starts(jax.random.fold_in(key_list[19], 71), 0)
    grad_out = gaussian(key_list[3], (TOKENS, D), 1.0, 6.0, ((0, 32),))
    attn_in = gaussian(key_list[4], (6, D, D), D ** -0.5, 0.1875, ((1, 8),), jnp.float32)
    attn_out = gaussian(key_list[5], (2, D, D), 2 ** -0.5, 4.0, ((1, 8),), jnp.float32)
    ffn_in = gaussian(key_list[6], (D, FF), D ** -0.5, 0.1875, ((0, 8),), jnp.float32)
    ffn_out = gaussian(key_list[7], (FF, D), FF ** -0.5, 0.0625, ((0, 8),), jnp.float32)
    norms = draw_norms(jax.random.fold_in(key_list[19], 71), 0)
    first_attn_in = gaussian(key_list[9], (6, D, D), 0.006, 0.036, ((1, 8),), jnp.float32)
    first_attn_out = gaussian(key_list[10], (2, D, D), 0.006, 0.036, ((1, 8),), jnp.float32)
    first_ffn_in = gaussian(key_list[11], (D, FF), 0.006, 0.036, ((0, 8),), jnp.float32)
    first_ffn_out = gaussian(key_list[12], (FF, D), 0.006, 0.036, ((0, 8),), jnp.float32)
    first_norms = gaussian(key_list[13], (6, D), 0.006, 0.036, (), jnp.float32)
    second_attn_in = jnp.clip(jnp.exp(math.log(0.001) - 4.6051703 * jax.random.uniform(key_list[14], (6, D, D), jnp.float32) ** level_of(key_list[14], (6, D, D), ((1, 8),), -0.2, 0.2)), 9.999999747378752e-06, 0.001)
    second_attn_out = jnp.clip(jnp.exp(math.log(0.001) - 4.6051703 * jax.random.uniform(key_list[15], (2, D, D), jnp.float32) ** level_of(key_list[15], (2, D, D), ((1, 8),), -0.2, 0.2)), 9.999999747378752e-06, 0.001)
    second_ffn_in = jnp.clip(jnp.exp(math.log(0.001) - 4.6051703 * jax.random.uniform(key_list[16], (D, FF), jnp.float32) ** level_of(key_list[16], (D, FF), ((0, 8),), -0.2, 0.2)), 9.999999747378752e-06, 0.001)
    second_ffn_out = jnp.clip(jnp.exp(math.log(0.001) - 4.6051703 * jax.random.uniform(key_list[17], (FF, D), jnp.float32) ** level_of(key_list[17], (FF, D), ((0, 8),), -0.2, 0.2)), 9.999999747378752e-06, 0.001)
    second_norms = jnp.clip(jnp.exp(jax.random.uniform(key_list[18], (6, D), jnp.float32, math.log(9.999999747378752e-06), math.log(0.001))), 9.999999747378752e-06, 0.001)
    return dict(hidden=hidden, encoder=encoder, piece_starts=piece_starts, grad_out=grad_out, attn_in=attn_in, attn_out=attn_out, ffn_in=ffn_in, ffn_out=ffn_out, norms=norms, first_attn_in=first_attn_in, first_attn_out=first_attn_out, first_ffn_in=first_ffn_in, first_ffn_out=first_ffn_out, first_norms=first_norms, second_attn_in=second_attn_in, second_attn_out=second_attn_out, second_ffn_in=second_ffn_in, second_ffn_out=second_ffn_out, second_norms=second_norms)


@jax.custom_vjp
def low(v):
    return lax.optimization_barrier(v.astype(jnp.bfloat16)).astype(jnp.float32)

@jax.custom_vjp
def low_back(v):
    return v

def low_keep(v):
    return (low(v), None)

def low_pass(kept, grad):
    return (grad,)

def back_keep(v):
    return (v, None)

def back_low(kept, grad):
    return (low(grad),)
low.defvjp(low_keep, low_pass)
low_back.defvjp(back_keep, back_low)
HIGH = lax.Precision.HIGHEST
NORM_EPS = 1e-05
SCALE = 0.125
BETA_ONE = 0.9
BETA_TWO = 0.95
CORRECT_ONE = 1.0 - 0.9 ** 8
CORRECT_TWO = 1.0 - 0.95 ** 8
ADAM_EPS = 1e-08
RATE = 0.01
DECAY = 0.1
CLIP_RMS = 0.05
CLIP_EPS = 1e-06

def matmul(left, right):
    return jnp.dot(left, right, precision=HIGH)

def both_round(value):
    return low(low_back(value))

def layer_norm(values_in, gain, shift):
    mean_val = lax.optimization_barrier(jnp.mean(values_in, axis=-1, keepdims=True))
    centred = values_in - mean_val
    variance = lax.optimization_barrier(jnp.mean(centred * centred, axis=-1, keepdims=True))
    return centred * lax.rsqrt(variance + NORM_EPS) * gain + shift

def piece_numbers(positions, starts):
    inside = (positions[:, None] >= starts[None, :]) & (positions[:, None] < starts[None, :] + PIECE_LEN)
    labels = jnp.arange(1, starts.shape[0] + 1, dtype=jnp.int32)
    return lax.optimization_barrier(jnp.sum(jnp.where(inside, labels[None, :], 0), axis=1)).astype(jnp.int32)

def attend(query_rows, key_rows, value_rows, visible):
    query_count = query_rows.shape[0]
    query_heads = query_rows.reshape(query_count, HEADS, HEAD_DIM)
    key_heads = key_rows.reshape(key_rows.shape[0], HEADS, HEAD_DIM)
    value_heads = value_rows.reshape(value_rows.shape[0], HEADS, HEAD_DIM)
    scores = low_back(jnp.einsum('bhd,khd->hbk', query_heads, key_heads, precision=HIGH) * SCALE)
    masked = jnp.where(visible[None], scores, -1e+30)
    row_peak = lax.optimization_barrier(jnp.max(masked, axis=-1, keepdims=True))
    exp_terms = jnp.where(visible[None], jnp.exp(masked - row_peak), 0.0)
    soft_weights = exp_terms / lax.optimization_barrier(jnp.sum(exp_terms, axis=-1, keepdims=True))
    head_out = jnp.einsum('hbk,khd->bhd', low(soft_weights), value_heads, precision=HIGH)
    return head_out.reshape(query_count, HEADS * HEAD_DIM)

def forward(params, hidden_seq, enc_seq, piece_ids):
    attn_in, attn_out, ffn_in, ffn_out, norms = [low(weight) for weight in params]
    positions = jnp.arange(SEQ_LEN, dtype=jnp.int32)
    block_size = math.gcd(SEQ_LEN, 512)
    block_count = SEQ_LEN // block_size
    normed_one = low(layer_norm(hidden_seq, norms[0], norms[1]))
    query_rows = both_round(matmul(normed_one, attn_in[0]))
    key_rows = both_round(matmul(normed_one, attn_in[1]))
    value_rows = both_round(matmul(normed_one, attn_in[2]))

    def self_block(block_item):
        rows_in, row_pos, row_ids = block_item
        visible = (positions[None, :] <= row_pos[:, None]) | (piece_ids[None, :] == row_ids[:, None]) & (row_ids[:, None] > 0)
        return attend(rows_in, key_rows, value_rows, visible)
    attended = lax.map(jax.checkpoint(self_block), (query_rows.reshape(block_count, block_size, D), positions.reshape(block_count, block_size), piece_ids.reshape(block_count, block_size)))
    attended = both_round(attended.reshape(SEQ_LEN, D))
    first_sum = hidden_seq + low_back(matmul(attended, attn_out[0]))
    normed_two = low(layer_norm(first_sum, norms[2], norms[3]))
    cross_queries = both_round(matmul(normed_two, attn_in[3]))
    cross_keys = both_round(matmul(enc_seq, attn_in[4]))
    cross_values = both_round(matmul(enc_seq, attn_in[5]))

    def cross_block(rows_in):
        visible = jnp.ones((rows_in.shape[0], ENC), dtype=jnp.bool_)
        return attend(rows_in, cross_keys, cross_values, visible)
    crossed = lax.map(jax.checkpoint(cross_block), cross_queries.reshape(block_count, block_size, D))
    crossed = both_round(crossed.reshape(SEQ_LEN, D))
    second_sum = first_sum + low_back(matmul(crossed, attn_out[1]))
    normed_three = low(layer_norm(second_sum, norms[4], norms[5]))
    pre_act = low_back(matmul(normed_three, ffn_in))
    activated = low(jax.nn.gelu(pre_act, approximate=True))
    return second_sum + low_back(matmul(activated, ffn_out))

def clip_units(grad):
    mean_sq = lax.optimization_barrier(jnp.mean(grad * grad, axis=-1, keepdims=True))
    return grad * jnp.minimum(1.0, CLIP_RMS * lax.rsqrt(mean_sq + CLIP_EPS))

def adam_update(weight, grad_sum, first_moment, second_moment):
    clipped = clip_units(grad_sum)
    first_new = BETA_ONE * first_moment + (1.0 - BETA_ONE) * clipped
    second_new = BETA_TWO * second_moment + (1.0 - BETA_TWO) * clipped * clipped
    step_size = first_new / CORRECT_ONE / (jnp.sqrt(second_new / CORRECT_TWO) + ADAM_EPS)
    return (first_new, second_new, -RATE * (step_size + DECAY * weight))

def reference(hidden, encoder, piece_starts, grad_out, attn_in, attn_out, ffn_in, ffn_out, norms, first_attn_in, first_attn_out, first_ffn_in, first_ffn_out, first_norms, second_attn_in, second_attn_out, second_ffn_in, second_ffn_out, second_norms):
    params = (attn_in, attn_out, ffn_in, ffn_out, norms)
    positions = jnp.arange(SEQ_LEN, dtype=jnp.int32)
    hidden_all = hidden.astype(jnp.float32).reshape(GROUPS, SEQ_LEN, D)
    enc_all = encoder.astype(jnp.float32).reshape(GROUPS, ENC, D)
    cot_all = grad_out.astype(jnp.float32).reshape(GROUPS, SEQ_LEN, D)

    def one_group(totals, group_item):
        hidden_seq, enc_seq, starts_seq, cot_seq = group_item
        piece_ids = piece_numbers(positions, starts_seq)

        def run_layer(weights, hidden_in, enc_in):
            return forward(weights, hidden_in, enc_in, piece_ids)
        result, pullback = jax.vjp(run_layer, params, hidden_seq, enc_seq)
        weight_grads, hidden_grad, enc_grad = pullback(cot_seq)
        totals = jax.tree.map(lambda left, right: left + right, totals, weight_grads)
        return (totals, (result, hidden_grad, enc_grad))
    zero_grads = jax.tree.map(jnp.zeros_like, params)
    totals, (results, hidden_grads, enc_grads) = lax.scan(one_group, zero_grads, (hidden_all, enc_all, piece_starts, cot_all))
    grad_scale = 1.0 / math.sqrt(TOKENS)
    weight_sums = [each_total * grad_scale for each_total in totals]
    firsts = (first_attn_in, first_attn_out, first_ffn_in, first_ffn_out, first_norms)
    seconds = (second_attn_in, second_attn_out, second_ffn_in, second_ffn_out, second_norms)
    updated = [adam_update(params[index], weight_sums[index], firsts[index], seconds[index]) for index in range(5)]
    return (results.reshape(TOKENS, D), hidden_grads.reshape(TOKENS, D), enc_grads.reshape(GROUPS * ENC, D), weight_sums[0], weight_sums[1], weight_sums[2], weight_sums[3], weight_sums[4], updated[0][0], updated[1][0], updated[2][0], updated[3][0], updated[4][0], updated[0][1], updated[1][1], updated[2][1], updated[3][1], updated[4][1], updated[0][2], updated[1][2], updated[2][2], updated[3][2], updated[4][2])
```

```python
import functools
import math

import jax
import jax.numpy as jnp
from jax import lax
from jax.experimental import pallas as pl
from jax.experimental.pallas import tpu as pltpu
from jax.sharding import Mesh
from jax.sharding import PartitionSpec as P

HEAD_DIM = 64
PIECE_LEN = 256

NORM_EPS = 1e-05
SCALE = 0.125
BETA_ONE = 0.9
BETA_TWO = 0.95
CORRECT_ONE = 1.0 - 0.9**8
CORRECT_TWO = 1.0 - 0.95**8
ADAM_EPS = 1e-08
RATE = 0.01
DECAY = 0.1
CLIP_RMS = 0.05
CLIP_EPS = 1e-06
MASKED = -1e30

SEQ = ("chip", "core")
BF16 = jnp.bfloat16
F32 = jnp.float32
VMEM_LIMIT = 48 * 1024 * 1024
NT = (((1,), (1,)), ((), ()))
TN = (((0,), (0,)), ((), ()))


def layer_norm(values_in, gain, shift):
    mean_val = jnp.mean(values_in, axis=-1, keepdims=True)
    centred = values_in - mean_val
    variance = jnp.mean(centred * centred, axis=-1, keepdims=True)
    return centred * lax.rsqrt(variance + NORM_EPS) * gain + shift


def dot_f32(left, right):
    return jnp.dot(left, right, preferred_element_type=F32)


def dot_nt(left, right):
    return lax.dot_general(left, right, NT, preferred_element_type=F32)


def dot_tn(left, right):
    return lax.dot_general(left, right, TN, preferred_element_type=F32)


def key_limit(positions, starts_ref, pieces):
    limit = positions + 1
    for piece in range(pieces):
        start = starts_ref[0, piece]
        inside = (positions >= start) & (positions < start + PIECE_LEN)
        limit = jnp.where(inside, jnp.maximum(limit, start + PIECE_LEN), limit)
    return limit


def spills_over(boundary, starts_ref, pieces):
    over = jnp.bool_(False)
    for piece in range(pieces):
        start = starts_ref[0, piece]
        over = over | ((start < boundary) & (start + PIECE_LEN > boundary))
    return over


def self_fwd_kernel(heads, pieces, block, starts_ref, q_ref, k_ref, v_ref, o_ref, lse_ref, s_ref):
    step = pl.program_id(0)
    last = pl.num_programs(0) - 1
    row_pos = step * block + lax.broadcasted_iota(jnp.int32, (block, 1), 0)
    limit = key_limit(row_pos, starts_ref, pieces)
    over = spills_over((step + 1) * block, starts_ref, pieces) & (step < last)
    blocks = step + 1 + over.astype(jnp.int32)
    for head in range(heads):
        cols = slice(head * HEAD_DIM, (head + 1) * HEAD_DIM)
        query = q_ref[:, cols] * BF16(SCALE)

        def scores(index):
            rows = pl.ds(pl.multiple_of(index * block, block), block)
            return dot_nt(query, k_ref[rows, cols])

        def masked_scores(index):
            key_pos = index * block + lax.broadcasted_iota(jnp.int32, (1, block), 1)
            return jnp.where(key_pos < limit, scores(index), MASKED)

        def lane_max(peak, values):
            for at in range(0, block, 128):
                peak = jnp.maximum(peak, values[:, at : at + 128])
            return peak

        def first_pass(index, peak):
            values = scores(index)
            s_ref[index] = values
            return lane_max(peak, values)

        def edge_pass(index, peak):
            values = masked_scores(index)
            s_ref[index] = values
            return lane_max(peak, values)

        peak = jnp.full((block, 128), MASKED, F32)
        peak = lax.fori_loop(0, step, first_pass, peak)
        peak = lax.fori_loop(step, blocks, edge_pass, peak)
        peak = jnp.max(peak, axis=1, keepdims=True)

        def second_pass(index, carry):
            total, out = carry
            terms = jnp.exp(s_ref[index] - peak)
            for at in range(0, block, 128):
                total = total + terms[:, at : at + 128]
            rows = pl.ds(pl.multiple_of(index * block, block), block)
            return total, out + dot_f32(terms.astype(BF16), v_ref[rows, cols])

        total, out = lax.fori_loop(
            0,
            blocks,
            second_pass,
            (jnp.zeros((block, 128), F32), jnp.zeros((block, HEAD_DIM), F32)),
        )
        total = jnp.sum(total, axis=1, keepdims=True)
        o_ref[:, cols] = (out / total).astype(BF16)
        lse = jnp.broadcast_to(peak + jnp.log(total), (block, 128))
        lse_ref[head] = jnp.transpose(lse)[:8]


def self_forward(starts, query, key, value, block):
    tokens, width = query.shape
    heads = width // HEAD_DIM
    pieces = starts.shape[1]
    whole = pl.BlockSpec((tokens, width), lambda i, s: (0, 0))
    flops = 2 * 2 * heads * tokens * tokens * HEAD_DIM
    return pl.pallas_call(
        functools.partial(self_fwd_kernel, heads, pieces, block),
        out_shape=(
            jax.ShapeDtypeStruct((tokens, width), BF16),
            jax.ShapeDtypeStruct((heads, 8, tokens), F32),
        ),
        grid_spec=pltpu.PrefetchScalarGridSpec(
            num_scalar_prefetch=1,
            grid=(tokens // block,),
            in_specs=[pl.BlockSpec((block, width), lambda i, s: (i, 0)), whole, whole],
            out_specs=(
                pl.BlockSpec((block, width), lambda i, s: (i, 0)),
                pl.BlockSpec((heads, 8, block), lambda i, s: (0, 0, i)),
            ),
            scratch_shapes=[pltpu.VMEM((tokens // block, block, block), F32)],
        ),
        compiler_params=pltpu.CompilerParams(
            dimension_semantics=("arbitrary",), vmem_limit_bytes=VMEM_LIMIT
        ),
        cost_estimate=pl.CostEstimate(
            flops=flops, bytes_accessed=8 * tokens * width, transcendentals=heads * tokens * tokens
        ),
        name="self_forward",
    )(starts, query, key, value)


def self_bwd_kernel(
    heads,
    pieces,
    block,
    starts_ref,
    q_ref,
    k_ref,
    v_ref,
    o_ref,
    do_ref,
    lse_ref,
    dq_ref,
    dk_ref,
    dv_ref,
    dk_acc,
    dv_acc,
):
    step = pl.program_id(0)
    last = pl.num_programs(0) - 1

    @pl.when(step == 0)
    def _():
        dk_acc[...] = jnp.zeros_like(dk_acc)
        dv_acc[...] = jnp.zeros_like(dv_acc)

    col_pos = step * block + lax.broadcasted_iota(jnp.int32, (1, block), 1)
    limit = key_limit(col_pos, starts_ref, pieces)
    over = spills_over((step + 1) * block, starts_ref, pieces) & (step < last)
    blocks = step + 1 + over.astype(jnp.int32)
    for head in range(heads):
        cols = slice(head * HEAD_DIM, (head + 1) * HEAD_DIM)
        query = q_ref[:, cols] * BF16(SCALE)
        grad = do_ref[:, cols]
        product = grad.astype(F32) * o_ref[:, cols].astype(F32)
        delta = lax.dot_general(
            jnp.ones((8, HEAD_DIM), F32),
            product,
            NT,
            precision=lax.Precision.HIGHEST,
            preferred_element_type=F32,
        )[:1]
        lse = lse_ref[head][:1]

        def one_block(masked, index, dq):
            rows = pl.ds(pl.multiple_of(index * block, block), block)
            key = k_ref[rows, cols]
            scores = dot_nt(key, query)
            if masked:
                key_pos = index * block + lax.broadcasted_iota(jnp.int32, (block, 1), 0)
                scores = jnp.where(key_pos < limit, scores, MASKED)
            weights = jnp.exp(scores - lse)
            grad_weights = dot_nt(v_ref[rows, cols], grad)
            dv_acc[rows, cols] += dot_f32(weights.astype(BF16), grad)
            grad_scores = (weights * (grad_weights - delta)).astype(BF16)
            dk_acc[rows, cols] += dot_f32(grad_scores, query)
            return dq + dot_tn(grad_scores, key)

        dq = jnp.zeros((block, HEAD_DIM), F32)
        dq = lax.fori_loop(0, step, functools.partial(one_block, False), dq)
        dq = lax.fori_loop(step, blocks, functools.partial(one_block, True), dq)
        dq_ref[:, cols] = (dq * SCALE).astype(BF16)

    @pl.when(step == last)
    def _():
        dk_ref[...] = dk_acc[...].astype(BF16)
        dv_ref[...] = dv_acc[...].astype(BF16)


def self_backward(starts, query, key, value, out, grad, lse, block):
    tokens, width = query.shape
    heads = width // HEAD_DIM
    pieces = starts.shape[1]
    whole = pl.BlockSpec((tokens, width), lambda i, s: (0, 0))
    rows = pl.BlockSpec((block, width), lambda i, s: (i, 0))
    flops = 5 * 2 * heads * tokens * tokens * HEAD_DIM
    shape = jax.ShapeDtypeStruct((tokens, width), BF16)
    return pl.pallas_call(
        functools.partial(self_bwd_kernel, heads, pieces, block),
        out_shape=(shape, shape, shape),
        grid_spec=pltpu.PrefetchScalarGridSpec(
            num_scalar_prefetch=1,
            grid=(tokens // block,),
            in_specs=[
                rows,
                whole,
                whole,
                rows,
                rows,
                pl.BlockSpec((heads, 8, block), lambda i, s: (0, 0, i)),
            ],
            out_specs=(rows, whole, whole),
            scratch_shapes=[pltpu.VMEM((tokens, width), F32), pltpu.VMEM((tokens, width), F32)],
        ),
        compiler_params=pltpu.CompilerParams(
            dimension_semantics=("arbitrary",), vmem_limit_bytes=VMEM_LIMIT
        ),
        cost_estimate=pl.CostEstimate(
            flops=flops, bytes_accessed=16 * tokens * width, transcendentals=heads * tokens * tokens
        ),
        name="self_backward",
    )(starts, query, key, value, out, grad, lse)


def cross_fwd_kernel(q_ref, k_ref, v_ref, o_ref, lse_ref):
    rows = q_ref.shape[0]
    for head in range(q_ref.shape[1] // HEAD_DIM):
        cols = slice(head * HEAD_DIM, (head + 1) * HEAD_DIM)
        scores = dot_nt(q_ref[:, cols] * BF16(SCALE), k_ref[:, cols])
        peak = jnp.max(scores, axis=1, keepdims=True)
        terms = jnp.exp(scores - peak)
        total = jnp.sum(terms, axis=1, keepdims=True)
        o_ref[:, cols] = (dot_f32(terms.astype(BF16), v_ref[:, cols]) / total).astype(BF16)
        lse = jnp.broadcast_to(peak + jnp.log(total), (rows, 128))
        lse_ref[head] = jnp.transpose(lse)[:8]


def cross_forward(query, key_value):
    rows, width = query.shape
    keys = key_value.shape[1]
    heads = width // HEAD_DIM
    return pl.pallas_call(
        lambda q, k, v, o, lse: cross_fwd_kernel(q, k, v, o, lse),
        out_shape=(
            jax.ShapeDtypeStruct((rows, width), BF16),
            jax.ShapeDtypeStruct((heads, 8, rows), F32),
        ),
        grid=(width // 128,),
        in_specs=[
            pl.BlockSpec((rows, 128), lambda i: (0, i)),
            pl.BlockSpec((None, keys, 128), lambda i: (0, 0, i)),
            pl.BlockSpec((None, keys, 128), lambda i: (1, 0, i)),
        ],
        out_specs=(
            pl.BlockSpec((rows, 128), lambda i: (0, i)),
            pl.BlockSpec((2, 8, rows), lambda i: (i, 0, 0)),
        ),
        compiler_params=pltpu.CompilerParams(
            dimension_semantics=("arbitrary",), vmem_limit_bytes=VMEM_LIMIT
        ),
        cost_estimate=pl.CostEstimate(
            flops=4 * rows * keys * width,
            bytes_accessed=4 * rows * width + 4 * keys * width,
            transcendentals=heads * rows * keys,
        ),
        name="cross_forward",
    )(query, key_value, key_value)


def cross_bwd_kernel(q_ref, k_ref, v_ref, o_ref, do_ref, lse_ref, dq_ref, dkv_ref):
    for head in range(q_ref.shape[1] // HEAD_DIM):
        cols = slice(head * HEAD_DIM, (head + 1) * HEAD_DIM)
        query = q_ref[:, cols] * BF16(SCALE)
        grad = do_ref[:, cols]
        product = grad.astype(F32) * o_ref[:, cols].astype(F32)
        delta = lax.dot_general(
            jnp.ones((8, HEAD_DIM), F32),
            product,
            NT,
            precision=lax.Precision.HIGHEST,
            preferred_element_type=F32,
        )[:1]
        key = k_ref[:, cols]
        weights = jnp.exp(dot_nt(key, query) - lse_ref[head][:1])
        grad_weights = dot_nt(v_ref[:, cols], grad)
        dkv_ref[1, :, cols] = dot_f32(weights.astype(BF16), grad).astype(BF16)
        grad_scores = (weights * (grad_weights - delta)).astype(BF16)
        dkv_ref[0, :, cols] = dot_f32(grad_scores, query).astype(BF16)
        dq_ref[:, cols] = (dot_tn(grad_scores, key) * SCALE).astype(BF16)


def cross_backward(query, key_value, out, grad, lse):
    rows, width = query.shape
    keys = key_value.shape[1]
    heads = width // HEAD_DIM
    rows_spec = pl.BlockSpec((rows, 128), lambda i: (0, i))
    return pl.pallas_call(
        lambda *refs: cross_bwd_kernel(*refs),
        out_shape=(
            jax.ShapeDtypeStruct((rows, width), BF16),
            jax.ShapeDtypeStruct((2, keys, width), BF16),
        ),
        grid=(width // 128,),
        in_specs=[
            rows_spec,
            pl.BlockSpec((None, keys, 128), lambda i: (0, 0, i)),
            pl.BlockSpec((None, keys, 128), lambda i: (1, 0, i)),
            rows_spec,
            rows_spec,
            pl.BlockSpec((2, 8, rows), lambda i: (i, 0, 0)),
        ],
        out_specs=(rows_spec, pl.BlockSpec((2, keys, 128), lambda i: (0, 0, i))),
        compiler_params=pltpu.CompilerParams(
            dimension_semantics=("arbitrary",), vmem_limit_bytes=VMEM_LIMIT
        ),
        cost_estimate=pl.CostEstimate(
            flops=10 * rows * keys * width,
            bytes_accessed=8 * rows * width + 8 * keys * width,
            transcendentals=heads * rows * keys,
        ),
        name="cross_backward",
    )(query, key_value, key_value, out, grad, lse)


def dp_swap(values, offset):
    count = lax.axis_size("dp")
    return lax.ppermute(values, "dp", [(index, index ^ offset) for index in range(count)])


def dp_gather(values):
    return [values] + [dp_swap(values, k) for k in range(1, lax.axis_size("dp"))]


def dp_scatter(blocks):
    total = blocks[0]
    for k in range(1, len(blocks)):
        total = total + dp_swap(blocks[k].astype(BF16), k).astype(F32)
    return total


def dp_join(values):
    copies = jnp.broadcast_to(values[None], (lax.axis_size("dp"),) + values.shape)
    return lax.all_to_all(copies, "dp", split_axis=0, concat_axis=0, tiled=True)


def own_part(values, axis):
    return lax.dynamic_index_in_dim(values, lax.axis_index("dp"), axis, keepdims=False)


def clip_units(grad):
    mean_sq = jnp.mean(grad * grad, axis=-1, keepdims=True)
    return grad * jnp.minimum(1.0, CLIP_RMS * lax.rsqrt(mean_sq + CLIP_EPS))


def adam_update(weight, grad_sum, first_moment, second_moment):
    clipped = clip_units(grad_sum)
    first_new = BETA_ONE * first_moment + (1.0 - BETA_ONE) * clipped
    second_new = BETA_TWO * second_moment + (1.0 - BETA_TWO) * clipped * clipped
    step_size = first_new / CORRECT_ONE / (jnp.sqrt(second_new / CORRECT_TWO) + ADAM_EPS)
    return (first_new, second_new, -RATE * (step_size + DECAY * weight))


def gelu_both(values_in):
    root = math.sqrt(2.0 / math.pi)
    square = values_in * values_in
    bent = jnp.tanh(root * (values_in + 0.044715 * values_in * square))
    half = 0.5 * (1.0 + bent)
    slope = half + 0.5 * values_in * (1.0 - bent * bent) * root * (1.0 + 3.0 * 0.044715 * square)
    return values_in * half, slope


def on_device(
    hidden,
    encoder,
    piece_starts,
    grad_out,
    attn_in,
    attn_out,
    ffn_in,
    ffn_out,
    norms,
    first_attn_in,
    first_attn_out,
    first_ffn_in,
    first_ffn_out,
    first_norms,
    second_attn_in,
    second_attn_out,
    second_ffn_in,
    second_ffn_out,
    second_norms,
):
    groups = lax.axis_size("dp")
    shards = lax.axis_size("chip") * lax.axis_size("core")
    rows, model = hidden.shape
    tokens = rows * shards
    width = model // shards
    shard_rows = attn_in.shape[1]
    part_rows = shard_rows // groups
    hidden_units = ffn_in.shape[1]
    unit_cut = hidden_units // (shards * groups)
    block = min(512, tokens)

    gains = lax.optimization_barrier(norms.astype(BF16)).astype(F32)
    resid_in = hidden.astype(F32)
    normed_one, norm_one_back = jax.vjp(layer_norm, resid_in, gains[0], gains[1])
    normed_one = normed_one.astype(BF16)
    normed_all = lax.all_gather(normed_one, SEQ, axis=0, tiled=True)

    to_heads = attn_in[:3].astype(BF16).reshape(3, shard_rows, shards, width)
    to_heads = lax.all_to_all(to_heads, SEQ, split_axis=2, concat_axis=1, tiled=True)
    to_heads = to_heads.reshape(3, model, width)

    def row_part(weights):
        cut = weights.reshape(weights.shape[0], groups, part_rows, model)
        return own_part(cut, 1).astype(BF16)

    early = jnp.concatenate([row_part(attn_out), row_part(attn_in[3:])], axis=0)
    early = lax.all_gather(early, SEQ + ("dp",), axis=1, tiled=True)
    w_o, w_co, w_cq, w_ck, w_cv = [early[index] for index in range(5)]
    encoder_all = lax.all_gather(encoder, SEQ, axis=0, tiled=True)

    up = own_part(ffn_in.reshape(shard_rows, shards, groups, unit_cut), 2)
    up = up.reshape(shard_rows, shards * unit_cut).astype(BF16)
    w_up = lax.all_gather(up, SEQ, axis=0, tiled=True)
    down = own_part(ffn_out.reshape(groups, unit_cut, model), 0).astype(BF16)
    w_down = lax.all_gather(down, SEQ, axis=0, tiled=True)
    late = row_part(attn_in[:3])
    late = lax.all_gather(late, SEQ + ("dp",), axis=1, tiled=True)

    qkv = dot_f32(normed_all, jnp.concatenate([to_heads[i] for i in range(3)], axis=1))
    qkv = qkv.astype(BF16)
    query, key, value = [qkv[:, i * width : (i + 1) * width] for i in range(3)]
    out_heads, self_lse = self_forward(piece_starts, query, key, value, block)
    attended = lax.all_to_all(
        out_heads.reshape(shards, rows, width), SEQ, split_axis=0, concat_axis=0, tiled=True
    )
    attended = attended.transpose(1, 0, 2).reshape(rows, model)
    first_sum = resid_in + dot_f32(attended, w_o)

    normed_two, norm_two_back = jax.vjp(layer_norm, first_sum, gains[2], gains[3])
    normed_two = normed_two.astype(BF16)
    cross_queries = dot_f32(normed_two, w_cq).astype(BF16)
    cross_kv = jnp.stack([dot_f32(encoder_all, w_ck), dot_f32(encoder_all, w_cv)]).astype(BF16)
    crossed, cross_lse = cross_forward(cross_queries, cross_kv)
    second_sum = first_sum + dot_f32(crossed, w_co)

    normed_three, norm_three_back = jax.vjp(layer_norm, second_sum, gains[4], gains[5])
    normed_three = normed_three.astype(BF16)
    grad_tokens = jnp.concatenate(dp_gather(grad_out), axis=0)
    ffn_tokens = jnp.concatenate(dp_gather(normed_three), axis=0)
    activated, slope = gelu_both(dot_f32(ffn_tokens, w_up))
    activated = activated.astype(BF16)
    grad_pre = (dot_nt(grad_tokens, w_down) * slope).astype(BF16)
    partial = dot_nt(grad_pre, w_up)
    grad_normed_three = dp_scatter(
        [partial[k * rows : (k + 1) * rows] for k in range(groups)]
    )
    partial = dot_f32(activated, w_down)
    out_hidden = second_sum + dp_scatter(
        [partial[k * rows : (k + 1) * rows] for k in range(groups)]
    )
    grad_down = dot_tn(activated, grad_tokens).astype(BF16)
    grad_up = dot_tn(ffn_tokens, grad_pre).astype(BF16)
    grad_down = lax.psum_scatter(grad_down, SEQ, scatter_dimension=0, tiled=True)
    grad_up = lax.psum_scatter(grad_up, SEQ, scatter_dimension=0, tiled=True)

    norm_part, grad_gain_three, grad_shift_three = norm_three_back(grad_normed_three)
    grad_second = grad_out.astype(F32) + norm_part
    grad_cross_branch = grad_second.astype(BF16)
    grad_w_co = dot_tn(crossed, grad_cross_branch)
    grad_crossed = dot_nt(grad_cross_branch, w_co).astype(BF16)
    grad_cq, grad_ckv = cross_backward(
        cross_queries, cross_kv, crossed, grad_crossed, cross_lse
    )
    grad_ckv = lax.psum_scatter(grad_ckv, SEQ, scatter_dimension=1, tiled=True)
    grad_w_cq = dot_tn(normed_two, grad_cq)
    norm_part, grad_gain_two, grad_shift_two = norm_two_back(dot_nt(grad_cq, w_cq))
    grad_first = grad_second + norm_part
    grad_self_branch = grad_first.astype(BF16)
    grad_attended = dot_nt(grad_self_branch, w_o).astype(BF16)
    grad_heads = lax.all_to_all(
        grad_attended.reshape(rows, shards, width).transpose(1, 0, 2),
        SEQ,
        split_axis=0,
        concat_axis=0,
        tiled=True,
    ).reshape(tokens, width)
    grad_w_o = dot_tn(attended, grad_self_branch)
    grad_q, grad_k, grad_v = self_backward(
        piece_starts, query, key, value, out_heads, grad_heads, self_lse, block
    )
    grad_qkv = jnp.stack([grad_q, grad_k, grad_v])
    grad_rows = lax.all_to_all(
        grad_qkv.reshape(3, shards, rows, width), SEQ, split_axis=1, concat_axis=1, tiled=True
    )
    grad_rows = grad_rows.transpose(0, 2, 1, 3).reshape(3, rows, model)
    grad_normed_one = (
        dot_nt(grad_rows[0], late[0]) + dot_nt(grad_rows[1], late[1]) + dot_nt(grad_rows[2], late[2])
    )
    norm_part, grad_gain_one, grad_shift_one = norm_one_back(grad_normed_one)
    grad_hidden = grad_first + norm_part

    grad_w_ck = dot_tn(encoder, grad_ckv[0])
    grad_w_cv = dot_tn(encoder, grad_ckv[1])
    grad_encoder = dot_nt(grad_ckv[0], w_ck) + dot_nt(grad_ckv[1], w_cv)

    index = lax.axis_index("dp")

    def dp_parts(grad):
        axis = grad.ndim - 3
        blocks = [
            lax.dynamic_index_in_dim(grad, index ^ k, axis, keepdims=False) for k in range(groups)
        ]
        return dp_scatter(blocks)

    local = jnp.stack([grad_w_o, grad_w_co, grad_w_cq, grad_w_ck, grad_w_cv])
    local = dp_parts(local.reshape(5, shards, groups, part_rows, model)).astype(BF16)
    local = local.reshape(5, shards * part_rows, model)
    local = lax.psum_scatter(local, SEQ, scatter_dimension=1, tiled=True)
    headed = dot_tn(normed_all, jnp.concatenate([grad_q, grad_k, grad_v], axis=1))
    headed = dp_parts(headed.reshape(shards, groups, part_rows, 3 * width)).astype(BF16)
    headed = lax.all_to_all(headed, SEQ, split_axis=0, concat_axis=0, tiled=True)
    headed = headed.reshape(shards, part_rows, 3, width).transpose(2, 1, 0, 3)
    headed = headed.reshape(3, part_rows, model)

    scale = 1.0 / math.sqrt(tokens * groups)
    local = dp_join(local)
    headed = dp_join(headed)

    def whole_rows(parts):
        return parts.transpose(1, 0, 2, 3).reshape(parts.shape[1], shard_rows, model)

    sum_out = whole_rows(local[:, :2]).astype(F32) * scale
    sum_in = (
        jnp.concatenate([whole_rows(headed), whole_rows(local[:, 2:])], axis=0).astype(F32) * scale
    )
    sum_down = dp_join(grad_down).reshape(groups * unit_cut, model).astype(F32) * scale
    sum_up = dp_join(grad_up.reshape(shard_rows, shards, unit_cut))
    sum_up = sum_up.transpose(1, 2, 0, 3).reshape(shard_rows, hidden_units).astype(F32) * scale
    sum_norms = jnp.stack(
        [
            grad_gain_one,
            grad_shift_one,
            grad_gain_two,
            grad_shift_two,
            grad_gain_three,
            grad_shift_three,
        ]
    )
    norm_total = lax.psum(sum_norms * scale, ("dp",) + SEQ)

    upd_in = adam_update(attn_in, sum_in, first_attn_in, second_attn_in)
    upd_out = adam_update(attn_out, sum_out, first_attn_out, second_attn_out)
    upd_up = adam_update(ffn_in, sum_up, first_ffn_in, second_ffn_in)
    upd_down = adam_update(ffn_out, sum_down, first_ffn_out, second_ffn_out)
    upd_norms = adam_update(norms, norm_total, first_norms, second_norms)
    return (
        out_hidden,
        grad_hidden,
        grad_encoder,
        sum_in,
        sum_out,
        sum_up,
        sum_down,
        norm_total,
        upd_in[0],
        upd_out[0],
        upd_up[0],
        upd_down[0],
        upd_norms[0],
        upd_in[1],
        upd_out[1],
        upd_up[1],
        upd_down[1],
        upd_norms[1],
        upd_in[2],
        upd_out[2],
        upd_up[2],
        upd_down[2],
        upd_norms[2],
    )


def solution(mesh):
    groups, shards = mesh.shape["dp"], mesh.shape["seq"]
    split = Mesh(mesh.devices.reshape(groups, shards // 2, 2), ("dp",) + SEQ)
    token = P(("dp",) + SEQ, None)
    stacked = P(None, SEQ, None)
    flat = P(SEQ, None)
    params = (stacked, stacked, flat, flat, P())
    return jax.shard_map(
        on_device,
        mesh=split,
        in_specs=(token, token, P("dp", None), token) + params * 3,
        out_specs=(token, token, token) + params * 4,
        check_vma=False,
    )
```

```python
import functools
import math

import jax
import jax.numpy as jnp
from jax import lax
from jax.experimental import pallas as pl
from jax.experimental.pallas import tpu as pltpu
from jax.sharding import Mesh
from jax.sharding import PartitionSpec as P

HEAD_DIM = 64
PIECE_LEN = 256

NORM_EPS = 1e-05
SCALE = 0.125
BETA_ONE = 0.9
BETA_TWO = 0.95
CORRECT_ONE = 1.0 - 0.9**8
CORRECT_TWO = 1.0 - 0.95**8
ADAM_EPS = 1e-08
RATE = 0.01
DECAY = 0.1
CLIP_RMS = 0.05
CLIP_EPS = 1e-06
MASKED = -1e30

SEQ = ("chip", "core")
BF16 = jnp.bfloat16
F32 = jnp.float32
VMEM_LIMIT = 48 * 1024 * 1024
NT = (((1,), (1,)), ((), ()))
TN = (((0,), (0,)), ((), ()))


def layer_norm(values_in, gain, shift):
    mean_val = jnp.mean(values_in, axis=-1, keepdims=True)
    centred = values_in - mean_val
    variance = jnp.mean(centred * centred, axis=-1, keepdims=True)
    return centred * lax.rsqrt(variance + NORM_EPS) * gain + shift


def dot_f32(left, right):
    return jnp.dot(left, right, preferred_element_type=F32)


def dot_nt(left, right):
    return lax.dot_general(left, right, NT, preferred_element_type=F32)


def dot_tn(left, right):
    return lax.dot_general(left, right, TN, preferred_element_type=F32)


def key_limit(positions, starts_ref, pieces):
    limit = positions + 1
    for piece in range(pieces):
        start = starts_ref[0, piece]
        inside = (positions >= start) & (positions < start + PIECE_LEN)
        limit = jnp.where(inside, jnp.maximum(limit, start + PIECE_LEN), limit)
    return limit


def spills_over(boundary, starts_ref, pieces):
    over = jnp.bool_(False)
    for piece in range(pieces):
        start = starts_ref[0, piece]
        over = over | ((start < boundary) & (start + PIECE_LEN > boundary))
    return over


def self_fwd_kernel(heads, pieces, block, starts_ref, q_ref, k_ref, v_ref, o_ref, lse_ref, s_ref):
    step = pl.program_id(0)
    last = pl.num_programs(0) - 1
    row_pos = step * block + lax.broadcasted_iota(jnp.int32, (block, 1), 0)
    limit = key_limit(row_pos, starts_ref, pieces)
    over = spills_over((step + 1) * block, starts_ref, pieces) & (step < last)
    blocks = step + 1 + over.astype(jnp.int32)
    for head in range(heads):
        cols = slice(head * HEAD_DIM, (head + 1) * HEAD_DIM)
        query = q_ref[:, cols] * BF16(SCALE)

        def scores(index):
            rows = pl.ds(pl.multiple_of(index * block, block), block)
            return dot_nt(query, k_ref[rows, cols])

        def masked_scores(index):
            key_pos = index * block + lax.broadcasted_iota(jnp.int32, (1, block), 1)
            return jnp.where(key_pos < limit, scores(index), MASKED)

        def lane_max(peak, values):
            for at in range(0, block, 128):
                peak = jnp.maximum(peak, values[:, at : at + 128])
            return peak

        def first_pass(index, peak):
            values = scores(index)
            s_ref[index] = values
            return lane_max(peak, values)

        def edge_pass(index, peak):
            values = masked_scores(index)
            s_ref[index] = values
            return lane_max(peak, values)

        peak = jnp.full((block, 128), MASKED, F32)
        peak = lax.fori_loop(0, step, first_pass, peak)
        peak = lax.fori_loop(step, blocks, edge_pass, peak)
        peak = jnp.max(peak, axis=1, keepdims=True)

        def second_pass(index, carry):
            total, out = carry
            terms = jnp.exp(s_ref[index] - peak)
            for at in range(0, block, 128):
                total = total + terms[:, at : at + 128]
            rows = pl.ds(pl.multiple_of(index * block, block), block)
            return total, out + dot_f32(terms.astype(BF16), v_ref[rows, cols])

        total, out = lax.fori_loop(
            0,
            blocks,
            second_pass,
            (jnp.zeros((block, 128), F32), jnp.zeros((block, HEAD_DIM), F32)),
        )
        total = jnp.sum(total, axis=1, keepdims=True)
        o_ref[:, cols] = (out / total).astype(BF16)
        lse = jnp.broadcast_to(peak + jnp.log(total), (block, 128))
        lse_ref[head] = jnp.transpose(lse)[:8]


def self_forward(starts, query, key, value, block):
    tokens, width = query.shape
    heads = width // HEAD_DIM
    pieces = starts.shape[1]
    whole = pl.BlockSpec((tokens, width), lambda i, s: (0, 0))
    flops = 2 * 2 * heads * tokens * tokens * HEAD_DIM
    return pl.pallas_call(
        functools.partial(self_fwd_kernel, heads, pieces, block),
        out_shape=(
            jax.ShapeDtypeStruct((tokens, width), BF16),
            jax.ShapeDtypeStruct((heads, 8, tokens), F32),
        ),
        grid_spec=pltpu.PrefetchScalarGridSpec(
            num_scalar_prefetch=1,
            grid=(tokens // block,),
            in_specs=[pl.BlockSpec((block, width), lambda i, s: (i, 0)), whole, whole],
            out_specs=(
                pl.BlockSpec((block, width), lambda i, s: (i, 0)),
                pl.BlockSpec((heads, 8, block), lambda i, s: (0, 0, i)),
            ),
            scratch_shapes=[pltpu.VMEM((tokens // block, block, block), F32)],
        ),
        compiler_params=pltpu.CompilerParams(
            dimension_semantics=("arbitrary",), vmem_limit_bytes=VMEM_LIMIT
        ),
        cost_estimate=pl.CostEstimate(
            flops=flops, bytes_accessed=8 * tokens * width, transcendentals=heads * tokens * tokens
        ),
        name="self_forward",
    )(starts, query, key, value)


def self_bwd_kernel(
    heads,
    pieces,
    block,
    starts_ref,
    q_ref,
    k_ref,
    v_ref,
    o_ref,
    do_ref,
    lse_ref,
    flat_ref,
    dk_acc,
    dv_acc,
):
    step = pl.program_id(0)
    last = pl.num_programs(0) - 1
    width = dk_acc.shape[1]

    @pl.when(step == 0)
    def _():
        dk_acc[...] = jnp.zeros_like(dk_acc)
        dv_acc[...] = jnp.zeros_like(dv_acc)

    col_pos = step * block + lax.broadcasted_iota(jnp.int32, (1, block), 1)
    limit = key_limit(col_pos, starts_ref, pieces)
    over = spills_over((step + 1) * block, starts_ref, pieces) & (step < last)
    blocks = step + 1 + over.astype(jnp.int32)
    for head in range(heads):
        cols = slice(head * HEAD_DIM, (head + 1) * HEAD_DIM)
        query = q_ref[:, cols] * BF16(SCALE)
        grad = do_ref[:, cols]
        product = grad.astype(F32) * o_ref[:, cols].astype(F32)
        delta = lax.dot_general(
            jnp.ones((8, HEAD_DIM), F32),
            product,
            NT,
            precision=lax.Precision.HIGHEST,
            preferred_element_type=F32,
        )[:1]
        lse = lse_ref[head][:1]

        def one_block(masked, index, dq):
            rows = pl.ds(pl.multiple_of(index * block, block), block)
            key = k_ref[rows, cols]
            scores = dot_nt(key, query)
            if masked:
                key_pos = index * block + lax.broadcasted_iota(jnp.int32, (block, 1), 0)
                scores = jnp.where(key_pos < limit, scores, MASKED)
            weights = jnp.exp(scores - lse)
            grad_weights = dot_nt(v_ref[rows, cols], grad)
            dv_acc[rows, cols] += dot_f32(weights.astype(BF16), grad)
            grad_scores = (weights * (grad_weights - delta)).astype(BF16)
            dk_acc[rows, cols] += dot_f32(grad_scores, query)
            return dq + dot_tn(grad_scores, key)

        dq = jnp.zeros((block, HEAD_DIM), F32)
        dq = lax.fori_loop(0, step, functools.partial(one_block, False), dq)
        dq = lax.fori_loop(step, blocks, functools.partial(one_block, True), dq)
        dq = (dq * SCALE).astype(BF16)
        flat_ref[pl.ds(pl.multiple_of(step * block, block), block), cols] = dq

    @pl.when(step == last)
    def _():
        for which, acc in ((1, dk_acc), (2, dv_acc)):
            flat_ref[:, which * width : (which + 1) * width] = acc[...].astype(BF16)


def self_backward(starts, query, key, value, out, grad, lse, block):
    tokens, width = query.shape
    heads = width // HEAD_DIM
    pieces = starts.shape[1]
    whole = pl.BlockSpec((tokens, width), lambda i, s: (0, 0))
    rows = pl.BlockSpec((block, width), lambda i, s: (i, 0))
    flops = 5 * 2 * heads * tokens * tokens * HEAD_DIM
    return pl.pallas_call(
        functools.partial(self_bwd_kernel, heads, pieces, block),
        out_shape=jax.ShapeDtypeStruct((tokens, 3 * width), BF16),
        grid_spec=pltpu.PrefetchScalarGridSpec(
            num_scalar_prefetch=1,
            grid=(tokens // block,),
            in_specs=[
                rows,
                whole,
                whole,
                rows,
                rows,
                pl.BlockSpec((heads, 8, block), lambda i, s: (0, 0, i)),
            ],
            out_specs=pl.BlockSpec((tokens, 3 * width), lambda i, s: (0, 0)),
            scratch_shapes=[pltpu.VMEM((tokens, width), F32), pltpu.VMEM((tokens, width), F32)],
        ),
        compiler_params=pltpu.CompilerParams(
            dimension_semantics=("arbitrary",), vmem_limit_bytes=VMEM_LIMIT
        ),
        cost_estimate=pl.CostEstimate(
            flops=flops, bytes_accessed=16 * tokens * width, transcendentals=heads * tokens * tokens
        ),
        name="self_backward",
    )(starts, query, key, value, out, grad, lse)


def cross_fwd_kernel(q_ref, k_ref, v_ref, o_ref, lse_ref):
    rows = q_ref.shape[0]
    for head in range(q_ref.shape[1] // HEAD_DIM):
        cols = slice(head * HEAD_DIM, (head + 1) * HEAD_DIM)
        scores = dot_nt(q_ref[:, cols] * BF16(SCALE), k_ref[:, cols])
        peak = jnp.max(scores, axis=1, keepdims=True)
        terms = jnp.exp(scores - peak)
        total = jnp.sum(terms, axis=1, keepdims=True)
        o_ref[:, cols] = (dot_f32(terms.astype(BF16), v_ref[:, cols]) / total).astype(BF16)
        lse = jnp.broadcast_to(peak + jnp.log(total), (rows, 128))
        lse_ref[head] = jnp.transpose(lse)[:8]


def cross_forward(query, key_value):
    rows, width = query.shape
    keys = key_value.shape[1]
    heads = width // HEAD_DIM
    return pl.pallas_call(
        lambda q, k, v, o, lse: cross_fwd_kernel(q, k, v, o, lse),
        out_shape=(
            jax.ShapeDtypeStruct((rows, width), BF16),
            jax.ShapeDtypeStruct((heads, 8, rows), F32),
        ),
        grid=(width // 128,),
        in_specs=[
            pl.BlockSpec((rows, 128), lambda i: (0, i)),
            pl.BlockSpec((None, keys, 128), lambda i: (0, 0, i)),
            pl.BlockSpec((None, keys, 128), lambda i: (1, 0, i)),
        ],
        out_specs=(
            pl.BlockSpec((rows, 128), lambda i: (0, i)),
            pl.BlockSpec((2, 8, rows), lambda i: (i, 0, 0)),
        ),
        compiler_params=pltpu.CompilerParams(
            dimension_semantics=("arbitrary",), vmem_limit_bytes=VMEM_LIMIT
        ),
        cost_estimate=pl.CostEstimate(
            flops=4 * rows * keys * width,
            bytes_accessed=4 * rows * width + 4 * keys * width,
            transcendentals=heads * rows * keys,
        ),
        name="cross_forward",
    )(query, key_value, key_value)


def cross_bwd_kernel(width, q_ref, k_ref, v_ref, o_ref, do_ref, lse_ref, dq_ref, dkv_ref):
    for head in range(q_ref.shape[1] // HEAD_DIM):
        cols = slice(head * HEAD_DIM, (head + 1) * HEAD_DIM)
        owner = head * HEAD_DIM // width
        own_cols = slice(head * HEAD_DIM % width, head * HEAD_DIM % width + HEAD_DIM)
        query = q_ref[:, cols] * BF16(SCALE)
        grad = do_ref[:, cols]
        product = grad.astype(F32) * o_ref[:, cols].astype(F32)
        delta = lax.dot_general(
            jnp.ones((8, HEAD_DIM), F32),
            product,
            NT,
            precision=lax.Precision.HIGHEST,
            preferred_element_type=F32,
        )[:1]
        key = k_ref[:, cols]
        weights = jnp.exp(dot_nt(key, query) - lse_ref[head][:1])
        grad_weights = dot_nt(v_ref[:, cols], grad)
        dkv_ref[owner, 1, :, own_cols] = dot_f32(weights.astype(BF16), grad).astype(BF16)
        grad_scores = (weights * (grad_weights - delta)).astype(BF16)
        dkv_ref[owner, 0, :, own_cols] = dot_f32(grad_scores, query).astype(BF16)
        dq_ref[:, cols] = (dot_tn(grad_scores, key) * SCALE).astype(BF16)


def cross_backward(query, key_value, out, grad, lse, owner_width):
    rows, width = query.shape
    keys = key_value.shape[1]
    heads = width // HEAD_DIM
    rows_spec = pl.BlockSpec((rows, 128), lambda i: (0, i))
    dkv_block = (128 // owner_width, 2, keys, owner_width)
    return pl.pallas_call(
        functools.partial(cross_bwd_kernel, owner_width),
        out_shape=(
            jax.ShapeDtypeStruct((rows, width), BF16),
            jax.ShapeDtypeStruct((width // owner_width, 2, keys, owner_width), BF16),
        ),
        grid=(width // 128,),
        in_specs=[
            rows_spec,
            pl.BlockSpec((None, keys, 128), lambda i: (0, 0, i)),
            pl.BlockSpec((None, keys, 128), lambda i: (1, 0, i)),
            rows_spec,
            rows_spec,
            pl.BlockSpec((2, 8, rows), lambda i: (i, 0, 0)),
        ],
        out_specs=(rows_spec, pl.BlockSpec(dkv_block, lambda i: (i, 0, 0, 0))),
        compiler_params=pltpu.CompilerParams(
            dimension_semantics=("arbitrary",), vmem_limit_bytes=VMEM_LIMIT
        ),
        cost_estimate=pl.CostEstimate(
            flops=10 * rows * keys * width,
            bytes_accessed=8 * rows * width + 8 * keys * width,
            transcendentals=heads * rows * keys,
        ),
        name="cross_backward",
    )(query, key_value, key_value, out, grad, lse)


def swap(values, axis, offset):
    count = lax.axis_size(axis)
    return lax.ppermute(values, axis, [(index, index ^ offset) for index in range(count)])


def dp_gather(values):
    return [values] + [swap(values, "dp", k) for k in range(1, lax.axis_size("dp"))]


def swap_blocks(blocks, axis):
    return [blocks[0]] + [swap(blocks[k], axis, k) for k in range(1, len(blocks))]


def pick_blocks(values, axis_name, axis):
    index = lax.axis_index(axis_name)
    return [
        lax.dynamic_index_in_dim(values, index ^ k, axis, keepdims=False)
        for k in range(values.shape[axis])
    ]


def tree_sum(parts):
    parts = [part.astype(F32) for part in parts]
    while len(parts) > 1:
        parts = [parts[k] + parts[k + 1] for k in range(0, len(parts), 2)]
    return parts[0]


def sum_everywhere(values):
    for axis in ("core", "chip", "dp"):
        count = lax.axis_size(axis)
        values = tree_sum([values] + [swap(values, axis, k) for k in range(1, count)])
    return values


def position():
    return jnp.stack([lax.axis_index(axis) for axis in ("dp",) + SEQ]).astype(jnp.int32)


def place_kernel(store, at_ref, *refs):
    store(at_ref[0], at_ref[1], at_ref[2], refs[:-1], refs[-1])


def place(parts, store, shape, block=None, part_blocks=None):
    steps = 1 if block is None else shape[0]
    block = shape if block is None else block
    part_blocks = [part.shape for part in parts] if part_blocks is None else part_blocks

    def spec(dims):
        return pl.BlockSpec(dims, lambda i, at: (i,) + (0,) * (len(dims) - 1))

    return pl.pallas_call(
        functools.partial(place_kernel, store),
        out_shape=jax.ShapeDtypeStruct(shape, parts[0].dtype),
        grid_spec=pltpu.PrefetchScalarGridSpec(
            num_scalar_prefetch=1,
            grid=(steps,),
            in_specs=[spec(dims) for dims in part_blocks],
            out_specs=spec(block),
        ),
        compiler_params=pltpu.CompilerParams(
            dimension_semantics=("arbitrary",), vmem_limit_bytes=VMEM_LIMIT
        ),
        cost_estimate=pl.CostEstimate(
            flops=0, bytes_accessed=4 * math.prod(shape), transcendentals=0
        ),
        name="place",
    )(position(), *parts)


def join_parts(parts, axis):
    shape = parts[0].shape
    full = shape[:axis] + (len(parts),) + shape[axis:]

    def store(dp_index, chip, core, refs, out):
        for k, ref in enumerate(refs):
            if axis == 0:
                out[dp_index ^ k] = ref[...]
            else:
                for lead in range(shape[0]):
                    where = (lead,) + (slice(None),) * (axis - 1) + (dp_index ^ k,)
                    out[where] = ref[lead]

    return place(parts, store, full)


def join_columns(parts, cut):
    groups = len(parts)
    rows, columns = parts[0].shape
    if cut % 128:
        joined = jnp.zeros((groups, rows, columns // cut, cut), parts[0].dtype)
        for k, part in enumerate(parts):
            part = part.reshape(rows, columns // cut, cut)
            index = lax.axis_index("dp") ^ k
            joined = lax.dynamic_update_index_in_dim(joined, part, index, 0)
        return joined.transpose(1, 2, 0, 3).reshape(rows, columns * groups)

    def store(dp_index, chip, core, refs, out):
        for k, ref in enumerate(refs):
            for s in range(columns // cut):
                start = pl.multiple_of((s * groups + (dp_index ^ k)) * cut, 128)
                out[:, pl.ds(start, cut)] = ref[:, s * cut : (s + 1) * cut]

    return place(parts, store, (rows, columns * groups))


def own_part(values, axis):
    return lax.dynamic_index_in_dim(values, lax.axis_index("dp"), axis, keepdims=False)


def fetch_columns(own):
    half = own.shape[1] // 2
    mine = lax.dynamic_slice_in_dim(own, lax.axis_index("core") * half, half, 1)
    return [swap(mine, "dp", k) for k in range(1, lax.axis_size("dp"))]


def share_columns(parts):
    return [swap(part, "core", 1) for part in parts]


def send_rows(parts):
    own, given = pick_blocks(parts, "core", 1)
    both = jnp.stack([own, swap(given, "core", 1)], axis=1)
    return swap_blocks(pick_blocks(both, "chip", 0), "chip")


def join_rows(parts):
    def store(dp_index, chip, core, refs, out):
        for k, ref in enumerate(refs):
            for flip in range(2):
                out[(chip ^ k) * 2 + (core ^ flip)] = ref[flip]

    return place(parts, store, (2 * len(parts),) + parts[0].shape[1:])


def join_fetched(parts):
    count, model, cut = parts[0].shape
    half = model // 2
    others = (len(parts) - 1) // 2

    def store(dp_index, chip, core, refs, out):
        out[0, :, pl.ds(pl.multiple_of(dp_index * cut, 128), cut)] = refs[0][0]
        for flip in range(2):
            rows = pl.ds(pl.multiple_of((core ^ flip) * half, 128), half)
            for k in range(1, others + 1):
                columns = pl.ds(pl.multiple_of((dp_index ^ k) * cut, 128), cut)
                out[0, rows, columns] = refs[flip * others + k][0]

    blocks = [(1,) + part.shape[1:] for part in parts]
    return place(parts, store, (count, model, model), (1, model, model), blocks)


def after(values, marker):
    return lax.optimization_barrier((values, marker))[0]


def meet(*values):
    return lax.optimization_barrier(values)


def take_columns_kernel(at_ref, in_ref, out_ref):
    out_ref[...] = in_ref[...].astype(BF16)


def take_columns(weights, shards, groups, cut):
    rows = weights.shape[0]
    if cut % 128:
        cut_up = own_part(weights.reshape(rows, shards, groups, cut), 2)
        return cut_up.reshape(rows, shards * cut).astype(BF16)
    return pl.pallas_call(
        take_columns_kernel,
        out_shape=jax.ShapeDtypeStruct((rows, shards * cut), BF16),
        grid_spec=pltpu.PrefetchScalarGridSpec(
            num_scalar_prefetch=1,
            grid=(shards,),
            in_specs=[pl.BlockSpec((rows, cut), lambda s, at: (0, s * groups + at[0]))],
            out_specs=pl.BlockSpec((rows, cut), lambda s, at: (0, s)),
        ),
        cost_estimate=pl.CostEstimate(
            flops=0, bytes_accessed=6 * rows * shards * cut, transcendentals=0
        ),
        name="take_columns",
    )(lax.axis_index("dp").astype(jnp.int32)[None], weights)


def clip_units(grad):
    mean_sq = jnp.mean(grad * grad, axis=-1, keepdims=True)
    return grad * jnp.minimum(1.0, CLIP_RMS * lax.rsqrt(mean_sq + CLIP_EPS))


def adam_update(weight, grad_sum, first_moment, second_moment):
    clipped = clip_units(grad_sum)
    first_new = BETA_ONE * first_moment + (1.0 - BETA_ONE) * clipped
    second_new = BETA_TWO * second_moment + (1.0 - BETA_TWO) * clipped * clipped
    step_size = first_new / CORRECT_ONE / (jnp.sqrt(second_new / CORRECT_TWO) + ADAM_EPS)
    return (first_new, second_new, -RATE * (step_size + DECAY * weight))


def adam_kernel(scale, g_ref, w_ref, m1_ref, m2_ref, g_out, m1_out, m2_out, change_out):
    grad = g_ref[...].astype(F32) * scale
    g_out[...] = grad
    m1_out[...], m2_out[...], change_out[...] = adam_update(
        w_ref[...], grad, m1_ref[...], m2_ref[...]
    )


def adam_call(grad, scale, weight, first, second):
    shape = weight.shape
    columns = shape[-1]
    rows = math.prod(shape[:-1])
    step = min(rows, 262144 // columns)
    spec = pl.BlockSpec((step, columns), lambda i: (i, 0))
    flat = jax.ShapeDtypeStruct((rows, columns), F32)
    outs = pl.pallas_call(
        functools.partial(adam_kernel, scale),
        out_shape=(flat,) * 4,
        grid=(rows // step,),
        in_specs=[spec] * 4,
        out_specs=(spec,) * 4,
        compiler_params=pltpu.CompilerParams(
            dimension_semantics=("arbitrary",), vmem_limit_bytes=VMEM_LIMIT
        ),
        cost_estimate=pl.CostEstimate(
            flops=20 * rows * columns, bytes_accessed=30 * rows * columns, transcendentals=0
        ),
        name="adam",
    )(*[array.reshape(rows, columns) for array in (grad, weight, first, second)])
    return [array.reshape(shape) for array in outs]


def gelu_both(values_in):
    root = math.sqrt(2.0 / math.pi)
    square = values_in * values_in
    bent = jnp.tanh(root * (values_in + 0.044715 * values_in * square))
    half = 0.5 * (1.0 + bent)
    slope = half + 0.5 * values_in * (1.0 - bent * bent) * root * (1.0 + 3.0 * 0.044715 * square)
    return values_in * half, slope


def on_device(
    hidden,
    encoder,
    piece_starts,
    grad_out,
    attn_in,
    attn_out,
    ffn_in,
    ffn_out,
    norms,
    first_attn_in,
    first_attn_out,
    first_ffn_in,
    first_ffn_out,
    first_norms,
    second_attn_in,
    second_attn_out,
    second_ffn_in,
    second_ffn_out,
    second_norms,
):
    groups = lax.axis_size("dp")
    shards = lax.axis_size("chip") * lax.axis_size("core")
    rows, model = hidden.shape
    tokens = rows * shards
    width = model // shards
    shard_rows = attn_in.shape[1]
    part_rows = shard_rows // groups
    hidden_units = ffn_in.shape[1]
    unit_cut = hidden_units // (shards * groups)
    block = min(512, tokens)

    core = lax.axis_index("core")
    chips = shards // 2
    gains = lax.optimization_barrier(norms.astype(BF16)).astype(F32)
    resid_in = hidden.astype(F32)
    normed_one, norm_one_back = jax.vjp(layer_norm, resid_in, gains[0], gains[1])
    normed_one = normed_one.astype(BF16)
    normed_all = lax.all_gather(normed_one, SEQ, axis=0, tiled=True)

    to_heads = own_part(attn_in[:3].reshape(3, groups, part_rows, shards, width), 1).astype(BF16)
    to_heads = to_heads.transpose(2, 1, 0, 3).reshape(shards, part_rows, 3 * width)
    to_heads = lax.all_to_all(to_heads, SEQ, split_axis=0, concat_axis=0, tiled=True)
    to_heads = dp_gather(to_heads)
    grad_parts = dp_gather(grad_out)

    def column_part(weights):
        cut = weights.reshape(weights.shape[0], shard_rows, groups, model // groups)
        return own_part(cut, 2).astype(BF16)

    first = column_part(jnp.concatenate([attn_out[:1], attn_in[3:4]], axis=0))
    second = column_part(jnp.concatenate([attn_in[4:], attn_out[1:]], axis=0))
    enc_rows = encoder.shape[0]
    second = jnp.concatenate(
        [second, encoder.reshape(enc_rows, groups, model // groups).transpose(1, 0, 2)], axis=0
    )
    up = take_columns(ffn_in, shards, groups, unit_cut)
    down = own_part(ffn_out.reshape(groups, unit_cut, model), 0).astype(BF16)
    to_heads = join_parts(to_heads, 1).reshape(model, 3 * width)
    normed_all, to_heads, grad_parts, first, second, up, down = meet(
        normed_all, to_heads, grad_parts, first, second, up, down
    )

    first = lax.all_gather(first, SEQ, axis=1, tiled=True)
    qkv = dot_f32(normed_all, to_heads).astype(BF16)
    second = lax.all_gather(after(second, qkv), SEQ, axis=1, tiled=True)
    query, key, value = [qkv[:, i * width : (i + 1) * width] for i in range(3)]
    out_heads, self_lse = self_forward(piece_starts, query, key, value, block)
    out_heads, first = meet(out_heads, first)
    w_up = lax.all_gather(after(up, out_heads), SEQ, axis=0, tiled=True)
    first_parts = fetch_columns(first)
    attended = lax.all_to_all(
        out_heads.reshape(shards, rows, width), SEQ, split_axis=0, concat_axis=0, tiled=True
    )
    attended, first_parts = meet(attended, first_parts)
    w_down = lax.all_gather(after(down, attended), SEQ, axis=0, tiled=True)
    first_shared = share_columns(first_parts)
    attended = attended.transpose(1, 0, 2).reshape(rows, model)
    attended, first_shared, second = meet(attended, first_shared, second)
    second_parts = fetch_columns(second[:3])
    encoder_all = second[3:].transpose(1, 0, 2).reshape(enc_rows * shards, model)
    w_o, w_cq = join_fetched([first] + first_parts + first_shared)
    first_sum = resid_in + dot_f32(attended, w_o)

    normed_two, norm_two_back = jax.vjp(layer_norm, first_sum, gains[2], gains[3])
    normed_two = normed_two.astype(BF16)
    cross_queries = dot_f32(normed_two, w_cq).astype(BF16)
    cross_queries, second_parts = meet(cross_queries, second_parts)
    w_ck, w_cv, w_co = join_fetched([second[:3]] + second_parts + share_columns(second_parts))
    cross_kv = jnp.stack([dot_f32(encoder_all, w_ck), dot_f32(encoder_all, w_cv)]).astype(BF16)
    crossed, cross_lse = cross_forward(cross_queries, cross_kv)
    second_sum = first_sum + dot_f32(crossed, w_co)

    normed_three, norm_three_back = jax.vjp(layer_norm, second_sum, gains[4], gains[5])
    normed_three = normed_three.astype(BF16)
    ffn_tokens = jnp.concatenate(dp_gather(normed_three), axis=0)
    grad_tokens = jnp.concatenate(grad_parts, axis=0)
    activated, slope = gelu_both(dot_f32(ffn_tokens, w_up))
    activated = activated.astype(BF16)
    grad_pre = (dot_nt(grad_tokens, w_down) * slope).astype(BF16)
    partial = dot_nt(grad_pre, w_up).astype(BF16)
    grad_three = swap_blocks([partial[k * rows : (k + 1) * rows] for k in range(groups)], "dp")
    activated, grad_pre = after((activated, grad_pre), partial)
    grad_down = dot_tn(activated, grad_tokens).astype(BF16)
    grad_up = dot_tn(ffn_tokens, grad_pre).astype(BF16)
    grad_down = lax.psum_scatter(grad_down, SEQ, scatter_dimension=0, tiled=True)
    activated, grad_three = after((activated, grad_three), grad_up)
    grad_up = lax.psum_scatter(grad_up, SEQ, scatter_dimension=0, tiled=True)
    partial = dot_f32(activated, w_down)
    hidden_parts = [partial[:rows]] + [
        partial[k * rows : (k + 1) * rows].astype(BF16) for k in range(1, groups)
    ]
    grad_three, hidden_parts = meet(grad_three, hidden_parts)
    hidden_parts = swap_blocks(hidden_parts, "dp")

    norm_part, grad_gain_three, grad_shift_three = norm_three_back(tree_sum(grad_three))
    grad_second = grad_out.astype(F32) + norm_part
    grad_cross_branch = grad_second.astype(BF16)
    grad_crossed = dot_nt(grad_cross_branch, w_co).astype(BF16)
    grad_cq, grad_ckv = cross_backward(
        cross_queries, cross_kv, crossed, grad_crossed, cross_lse, width
    )
    grad_cq, hidden_parts, grad_ckv = meet(grad_cq, hidden_parts, grad_ckv)
    grad_ckv = lax.psum_scatter(grad_ckv, SEQ, scatter_dimension=0, tiled=True)
    grad_ckv = grad_ckv.reshape(2, enc_rows * shards, width)
    grad_normed_two = dot_nt(grad_cq, w_cq)
    norm_part, grad_gain_two, grad_shift_two = norm_two_back(grad_normed_two)
    grad_first = grad_second + norm_part
    grad_self_branch = grad_first.astype(BF16)
    grad_attended = dot_nt(grad_self_branch, w_o).astype(BF16)
    grad_heads = lax.all_to_all(
        grad_attended.reshape(rows, shards, width).transpose(1, 0, 2),
        SEQ,
        split_axis=0,
        concat_axis=0,
        tiled=True,
    ).reshape(tokens, width)

    crossed, attended, grad_down = after((crossed, attended, grad_down), grad_attended)
    down_parts = dp_gather(grad_down)
    grad_w_co = dot_tn(crossed, grad_cross_branch)
    grad_w_cq = dot_tn(normed_two, grad_cq)
    grad_w_o = dot_tn(attended, grad_self_branch)
    local = jnp.stack([grad.astype(BF16) for grad in (grad_w_o, grad_w_co, grad_w_cq)])
    local = swap_blocks(pick_blocks(local.reshape(3, chips, 2, shard_rows, model), "core", 2), "core")
    grad_heads, local, down_parts = meet(grad_heads, local, down_parts)

    def reduce_headed(inputs, grads):
        headed = dot_tn(inputs, grads).astype(BF16)
        headed = headed.reshape(shards, groups, part_rows, grads.shape[1])
        return swap_blocks(pick_blocks(headed, "dp", 1), "dp")

    def send_headed(headed):
        headed = tree_sum(headed).astype(BF16)
        return send_rows(headed.reshape(chips, 2, part_rows, headed.shape[2]))

    def headed_rows(headed):
        count = headed[0].shape[2] // width
        headed = join_rows(headed).reshape(shards, part_rows, count, width)
        return headed.transpose(2, 1, 0, 3).reshape(count, part_rows, model)

    local = tree_sum(local).astype(BF16).reshape(3, chips, groups, part_rows, model)
    local = swap_blocks(pick_blocks(local, "dp", 2), "dp")
    grad_flat = self_backward(
        piece_starts, query, key, value, out_heads, grad_heads, self_lse, block
    )
    grad_flat, local = meet(grad_flat, local)

    scale = 1.0 / math.sqrt(tokens * groups)
    partial = dot_nt(grad_flat, to_heads).astype(BF16)
    grad_flat, local, down_parts = after((grad_flat, local, down_parts), partial)
    grad_normed_one = lax.psum_scatter(partial, SEQ, scatter_dimension=0, tiled=True)
    self_part = reduce_headed(normed_all, grad_flat)
    whole_down = join_parts(down_parts, 0)
    local = pick_blocks(tree_sum(local).astype(BF16), "chip", 1)
    self_part, whole_down = meet(self_part, whole_down)
    local = swap_blocks(local, "chip")
    sum_down, *upd_down = adam_call(whole_down, scale, ffn_out, first_ffn_out, second_ffn_out)
    local, sum_down, grad_ckv, grad_up = meet(local, sum_down, grad_ckv, grad_up)
    cross_part = reduce_headed(encoder_all, jnp.concatenate([grad_ckv[0], grad_ckv[1]], axis=1))
    headed = send_headed(
        [jnp.concatenate([left, right], axis=2) for left, right in zip(self_part, cross_part)]
    )
    ckv_rows = lax.all_to_all(
        grad_ckv.reshape(2, shards, enc_rows, width).transpose(1, 0, 2, 3),
        SEQ,
        split_axis=0,
        concat_axis=0,
        tiled=True,
    )
    up_parts = dp_gather(after(grad_up, cross_part[0]))
    headed = headed_rows(headed)
    local = tree_sum(local).astype(BF16)
    up_parts, headed = meet(up_parts, headed)
    attn_parts = dp_gather(jnp.concatenate([headed[:3], local[2:], headed[3:], local[:2]]))
    whole_up = join_columns(up_parts, unit_cut)
    sum_up, *upd_up = adam_call(whole_up, scale, ffn_in, first_ffn_in, second_ffn_in)
    attn_parts, sum_up, ckv_rows = meet(attn_parts, sum_up, ckv_rows)
    whole_attn = join_parts(attn_parts, 1).reshape(8, shard_rows, model)
    ckv_rows = ckv_rows.transpose(1, 2, 0, 3).reshape(2, enc_rows, model)
    grad_encoder = dot_nt(ckv_rows[0], w_ck) + dot_nt(ckv_rows[1], w_cv)
    grad_normed_one = after(grad_normed_one, whole_attn).astype(F32)
    norm_part, grad_gain_one, grad_shift_one = norm_one_back(grad_normed_one)
    grad_hidden = grad_first + norm_part
    sum_norms = jnp.stack(
        [
            grad_gain_one,
            grad_shift_one,
            grad_gain_two,
            grad_shift_two,
            grad_gain_three,
            grad_shift_three,
        ]
    )
    norm_total = sum_everywhere(sum_norms * scale)
    sum_in, *upd_in = adam_call(whole_attn[:6], scale, attn_in, first_attn_in, second_attn_in)
    sum_out, *upd_out = adam_call(whole_attn[6:], scale, attn_out, first_attn_out, second_attn_out)
    upd_norms = adam_update(norms, norm_total, first_norms, second_norms)
    out_hidden = second_sum + tree_sum(hidden_parts)
    return (
        out_hidden,
        grad_hidden,
        grad_encoder,
        sum_in,
        sum_out,
        sum_up,
        sum_down,
        norm_total,
        upd_in[0],
        upd_out[0],
        upd_up[0],
        upd_down[0],
        upd_norms[0],
        upd_in[1],
        upd_out[1],
        upd_up[1],
        upd_down[1],
        upd_norms[1],
        upd_in[2],
        upd_out[2],
        upd_up[2],
        upd_down[2],
        upd_norms[2],
    )


def solution(mesh):
    groups, shards = mesh.shape["dp"], mesh.shape["seq"]
    split = Mesh(mesh.devices.reshape(groups, shards // 2, 2), ("dp",) + SEQ)
    token = P(("dp",) + SEQ, None)
    stacked = P(None, SEQ, None)
    flat = P(SEQ, None)
    params = (stacked, stacked, flat, flat, P())
    return jax.shard_map(
        on_device,
        mesh=split,
        in_specs=(token, token, P("dp", None), token) + params * 3,
        out_specs=(token, token, token) + params * 4,
        check_vma=False,
    )
```

```python
import functools
import math

import jax
import jax.numpy as jnp
from jax import lax
from jax.experimental import pallas as pl
from jax.experimental.pallas import tpu as pltpu
from jax.sharding import Mesh
from jax.sharding import PartitionSpec as P

HEAD_DIM = 64
PIECE_LEN = 256

NORM_EPS = 1e-05
SCALE = 0.125
BETA_ONE = 0.9
BETA_TWO = 0.95
CORRECT_ONE = 1.0 - 0.9**8
CORRECT_TWO = 1.0 - 0.95**8
ADAM_EPS = 1e-08
RATE = 0.01
DECAY = 0.1
CLIP_RMS = 0.05
CLIP_EPS = 1e-06
MASKED = -1e30

SEQ = ("chip", "core")
BF16 = jnp.bfloat16
F32 = jnp.float32
VMEM_LIMIT = 48 * 1024 * 1024
NT = (((1,), (1,)), ((), ()))
TN = (((0,), (0,)), ((), ()))


def layer_norm(values_in, gain, shift):
    mean_val = jnp.mean(values_in, axis=-1, keepdims=True)
    centred = values_in - mean_val
    variance = jnp.mean(centred * centred, axis=-1, keepdims=True)
    return centred * lax.rsqrt(variance + NORM_EPS) * gain + shift


def dot_f32(left, right):
    return jnp.dot(left, right, preferred_element_type=F32)


def dot_nt(left, right):
    return lax.dot_general(left, right, NT, preferred_element_type=F32)


def dot_tn(left, right):
    return lax.dot_general(left, right, TN, preferred_element_type=F32)


def key_limit(positions, starts_ref, pieces):
    limit = positions + 1
    for piece in range(pieces):
        start = starts_ref[0, piece]
        inside = (positions >= start) & (positions < start + PIECE_LEN)
        limit = jnp.where(inside, jnp.maximum(limit, start + PIECE_LEN), limit)
    return limit


def spills_over(boundary, starts_ref, pieces):
    over = jnp.bool_(False)
    for piece in range(pieces):
        start = starts_ref[0, piece]
        over = over | ((start < boundary) & (start + PIECE_LEN > boundary))
    return over


def self_fwd_kernel(heads, pieces, block, starts_ref, q_ref, k_ref, v_ref, o_ref, lse_ref, s_ref):
    step = pl.program_id(0)
    last = pl.num_programs(0) - 1
    row_pos = step * block + lax.broadcasted_iota(jnp.int32, (block, 1), 0)
    limit = key_limit(row_pos, starts_ref, pieces)
    over = spills_over((step + 1) * block, starts_ref, pieces) & (step < last)
    blocks = step + 1 + over.astype(jnp.int32)
    for head in range(heads):
        cols = slice(head * HEAD_DIM, (head + 1) * HEAD_DIM)
        query = q_ref[:, cols] * BF16(SCALE)

        def scores(index):
            rows = pl.ds(pl.multiple_of(index * block, block), block)
            return dot_nt(query, k_ref[rows, cols])

        def masked_scores(index):
            key_pos = index * block + lax.broadcasted_iota(jnp.int32, (1, block), 1)
            return jnp.where(key_pos < limit, scores(index), MASKED)

        def lane_max(peak, values):
            for at in range(0, block, 128):
                peak = jnp.maximum(peak, values[:, at : at + 128])
            return peak

        def first_pass(index, peak):
            values = scores(index)
            s_ref[index] = values
            return lane_max(peak, values)

        def edge_pass(index, peak):
            values = masked_scores(index)
            s_ref[index] = values
            return lane_max(peak, values)

        peak = jnp.full((block, 128), MASKED, F32)
        peak = lax.fori_loop(0, step, first_pass, peak)
        peak = lax.fori_loop(step, blocks, edge_pass, peak)
        peak = jnp.max(peak, axis=1, keepdims=True)

        def second_pass(index, carry):
            total, out = carry
            terms = jnp.exp(s_ref[index] - peak)
            for at in range(0, block, 128):
                total = total + terms[:, at : at + 128]
            rows = pl.ds(pl.multiple_of(index * block, block), block)
            return total, out + dot_f32(terms.astype(BF16), v_ref[rows, cols])

        total, out = lax.fori_loop(
            0,
            blocks,
            second_pass,
            (jnp.zeros((block, 128), F32), jnp.zeros((block, HEAD_DIM), F32)),
        )
        total = jnp.sum(total, axis=1, keepdims=True)
        o_ref[:, cols] = (out / total).astype(BF16)
        lse = jnp.broadcast_to(peak + jnp.log(total), (block, 128))
        lse_ref[head] = jnp.transpose(lse)[:8]


def self_forward(starts, query, key, value, block):
    tokens, width = query.shape
    heads = width // HEAD_DIM
    pieces = starts.shape[1]
    whole = pl.BlockSpec((tokens, width), lambda i, s: (0, 0))
    flops = 2 * 2 * heads * tokens * tokens * HEAD_DIM
    return pl.pallas_call(
        functools.partial(self_fwd_kernel, heads, pieces, block),
        out_shape=(
            jax.ShapeDtypeStruct((tokens, width), BF16),
            jax.ShapeDtypeStruct((heads, 8, tokens), F32),
        ),
        grid_spec=pltpu.PrefetchScalarGridSpec(
            num_scalar_prefetch=1,
            grid=(tokens // block,),
            in_specs=[pl.BlockSpec((block, width), lambda i, s: (i, 0)), whole, whole],
            out_specs=(
                pl.BlockSpec((block, width), lambda i, s: (i, 0)),
                pl.BlockSpec((heads, 8, block), lambda i, s: (0, 0, i)),
            ),
            scratch_shapes=[pltpu.VMEM((tokens // block, block, block), F32)],
        ),
        compiler_params=pltpu.CompilerParams(
            dimension_semantics=("arbitrary",), vmem_limit_bytes=VMEM_LIMIT
        ),
        cost_estimate=pl.CostEstimate(
            flops=flops, bytes_accessed=8 * tokens * width, transcendentals=heads * tokens * tokens
        ),
        name="self_forward",
    )(starts, query, key, value)


def self_bwd_kernel(
    heads,
    pieces,
    block,
    starts_ref,
    q_ref,
    k_ref,
    v_ref,
    o_ref,
    do_ref,
    lse_ref,
    flat_ref,
    dk_acc,
    dv_acc,
):
    step = pl.program_id(0)
    last = pl.num_programs(0) - 1
    width = dk_acc.shape[1]

    @pl.when(step == 0)
    def _():
        dk_acc[...] = jnp.zeros_like(dk_acc)
        dv_acc[...] = jnp.zeros_like(dv_acc)

    col_pos = step * block + lax.broadcasted_iota(jnp.int32, (1, block), 1)
    limit = key_limit(col_pos, starts_ref, pieces)
    over = spills_over((step + 1) * block, starts_ref, pieces) & (step < last)
    blocks = step + 1 + over.astype(jnp.int32)
    for head in range(heads):
        cols = slice(head * HEAD_DIM, (head + 1) * HEAD_DIM)
        query = q_ref[:, cols] * BF16(SCALE)
        grad = do_ref[:, cols]
        product = grad.astype(F32) * o_ref[:, cols].astype(F32)
        delta = lax.dot_general(
            jnp.ones((8, HEAD_DIM), F32),
            product,
            NT,
            precision=lax.Precision.HIGHEST,
            preferred_element_type=F32,
        )[:1]
        lse = lse_ref[head][:1]

        def one_block(masked, index, dq):
            rows = pl.ds(pl.multiple_of(index * block, block), block)
            key = k_ref[rows, cols]
            scores = dot_nt(key, query)
            if masked:
                key_pos = index * block + lax.broadcasted_iota(jnp.int32, (block, 1), 0)
                scores = jnp.where(key_pos < limit, scores, MASKED)
            weights = jnp.exp(scores - lse)
            grad_weights = dot_nt(v_ref[rows, cols], grad)
            dv_acc[rows, cols] += dot_f32(weights.astype(BF16), grad)
            grad_scores = (weights * (grad_weights - delta)).astype(BF16)
            dk_acc[rows, cols] += dot_f32(grad_scores, query)
            return dq + dot_tn(grad_scores, key)

        dq = jnp.zeros((block, HEAD_DIM), F32)
        dq = lax.fori_loop(0, step, functools.partial(one_block, False), dq)
        dq = lax.fori_loop(step, blocks, functools.partial(one_block, True), dq)
        dq = (dq * SCALE).astype(BF16)
        flat_ref[pl.ds(pl.multiple_of(step * block, block), block), cols] = dq

    @pl.when(step == last)
    def _():
        for which, acc in ((1, dk_acc), (2, dv_acc)):
            flat_ref[:, which * width : (which + 1) * width] = acc[...].astype(BF16)


def self_backward(starts, query, key, value, out, grad, lse, block):
    tokens, width = query.shape
    heads = width // HEAD_DIM
    pieces = starts.shape[1]
    whole = pl.BlockSpec((tokens, width), lambda i, s: (0, 0))
    rows = pl.BlockSpec((block, width), lambda i, s: (i, 0))
    flops = 5 * 2 * heads * tokens * tokens * HEAD_DIM
    return pl.pallas_call(
        functools.partial(self_bwd_kernel, heads, pieces, block),
        out_shape=jax.ShapeDtypeStruct((tokens, 3 * width), BF16),
        grid_spec=pltpu.PrefetchScalarGridSpec(
            num_scalar_prefetch=1,
            grid=(tokens // block,),
            in_specs=[
                rows,
                whole,
                whole,
                rows,
                rows,
                pl.BlockSpec((heads, 8, block), lambda i, s: (0, 0, i)),
            ],
            out_specs=pl.BlockSpec((tokens, 3 * width), lambda i, s: (0, 0)),
            scratch_shapes=[pltpu.VMEM((tokens, width), F32), pltpu.VMEM((tokens, width), F32)],
        ),
        compiler_params=pltpu.CompilerParams(
            dimension_semantics=("arbitrary",), vmem_limit_bytes=VMEM_LIMIT
        ),
        cost_estimate=pl.CostEstimate(
            flops=flops, bytes_accessed=16 * tokens * width, transcendentals=heads * tokens * tokens
        ),
        name="self_backward",
    )(starts, query, key, value, out, grad, lse)


def cross_fwd_kernel(q_ref, k_ref, v_ref, o_ref, lse_ref):
    rows = q_ref.shape[0]
    for head in range(q_ref.shape[1] // HEAD_DIM):
        cols = slice(head * HEAD_DIM, (head + 1) * HEAD_DIM)
        scores = dot_nt(q_ref[:, cols] * BF16(SCALE), k_ref[:, cols])
        peak = jnp.max(scores, axis=1, keepdims=True)
        terms = jnp.exp(scores - peak)
        total = jnp.sum(terms, axis=1, keepdims=True)
        o_ref[:, cols] = (dot_f32(terms.astype(BF16), v_ref[:, cols]) / total).astype(BF16)
        lse = jnp.broadcast_to(peak + jnp.log(total), (rows, 128))
        lse_ref[head] = jnp.transpose(lse)[:8]


def cross_forward(query, key_value):
    rows, width = query.shape
    keys = key_value.shape[1]
    heads = width // HEAD_DIM
    return pl.pallas_call(
        lambda q, k, v, o, lse: cross_fwd_kernel(q, k, v, o, lse),
        out_shape=(
            jax.ShapeDtypeStruct((rows, width), BF16),
            jax.ShapeDtypeStruct((heads, 8, rows), F32),
        ),
        grid=(width // 128,),
        in_specs=[
            pl.BlockSpec((rows, 128), lambda i: (0, i)),
            pl.BlockSpec((None, keys, 128), lambda i: (0, 0, i)),
            pl.BlockSpec((None, keys, 128), lambda i: (1, 0, i)),
        ],
        out_specs=(
            pl.BlockSpec((rows, 128), lambda i: (0, i)),
            pl.BlockSpec((2, 8, rows), lambda i: (i, 0, 0)),
        ),
        compiler_params=pltpu.CompilerParams(
            dimension_semantics=("arbitrary",), vmem_limit_bytes=VMEM_LIMIT
        ),
        cost_estimate=pl.CostEstimate(
            flops=4 * rows * keys * width,
            bytes_accessed=4 * rows * width + 4 * keys * width,
            transcendentals=heads * rows * keys,
        ),
        name="cross_forward",
    )(query, key_value, key_value)


def cross_bwd_kernel(width, q_ref, k_ref, v_ref, o_ref, do_ref, lse_ref, dq_ref, dkv_ref):
    for head in range(q_ref.shape[1] // HEAD_DIM):
        cols = slice(head * HEAD_DIM, (head + 1) * HEAD_DIM)
        owner = head * HEAD_DIM // width
        own_cols = slice(head * HEAD_DIM % width, head * HEAD_DIM % width + HEAD_DIM)
        query = q_ref[:, cols] * BF16(SCALE)
        grad = do_ref[:, cols]
        product = grad.astype(F32) * o_ref[:, cols].astype(F32)
        delta = lax.dot_general(
            jnp.ones((8, HEAD_DIM), F32),
            product,
            NT,
            precision=lax.Precision.HIGHEST,
            preferred_element_type=F32,
        )[:1]
        key = k_ref[:, cols]
        weights = jnp.exp(dot_nt(key, query) - lse_ref[head][:1])
        grad_weights = dot_nt(v_ref[:, cols], grad)
        dkv_ref[owner, 1, :, own_cols] = dot_f32(weights.astype(BF16), grad).astype(BF16)
        grad_scores = (weights * (grad_weights - delta)).astype(BF16)
        dkv_ref[owner, 0, :, own_cols] = dot_f32(grad_scores, query).astype(BF16)
        dq_ref[:, cols] = (dot_tn(grad_scores, key) * SCALE).astype(BF16)


def cross_backward(query, key_value, out, grad, lse, owner_width):
    rows, width = query.shape
    keys = key_value.shape[1]
    heads = width // HEAD_DIM
    rows_spec = pl.BlockSpec((rows, 128), lambda i: (0, i))
    dkv_block = (128 // owner_width, 2, keys, owner_width)
    return pl.pallas_call(
        functools.partial(cross_bwd_kernel, owner_width),
        out_shape=(
            jax.ShapeDtypeStruct((rows, width), BF16),
            jax.ShapeDtypeStruct((width // owner_width, 2, keys, owner_width), BF16),
        ),
        grid=(width // 128,),
        in_specs=[
            rows_spec,
            pl.BlockSpec((None, keys, 128), lambda i: (0, 0, i)),
            pl.BlockSpec((None, keys, 128), lambda i: (1, 0, i)),
            rows_spec,
            rows_spec,
            pl.BlockSpec((2, 8, rows), lambda i: (i, 0, 0)),
        ],
        out_specs=(rows_spec, pl.BlockSpec(dkv_block, lambda i: (i, 0, 0, 0))),
        compiler_params=pltpu.CompilerParams(
            dimension_semantics=("arbitrary",), vmem_limit_bytes=VMEM_LIMIT
        ),
        cost_estimate=pl.CostEstimate(
            flops=10 * rows * keys * width,
            bytes_accessed=8 * rows * width + 8 * keys * width,
            transcendentals=heads * rows * keys,
        ),
        name="cross_backward",
    )(query, key_value, key_value, out, grad, lse)


def swap(values, axis, offset):
    count = lax.axis_size(axis)
    return lax.ppermute(values, axis, [(index, index ^ offset) for index in range(count)])


def dp_gather(values):
    return [values] + [swap(values, "dp", k) for k in range(1, lax.axis_size("dp"))]


def swap_blocks(blocks, axis):
    return [blocks[0]] + [swap(blocks[k], axis, k) for k in range(1, len(blocks))]


def pick_blocks(values, axis_name, axis):
    index = lax.axis_index(axis_name)
    return [
        lax.dynamic_index_in_dim(values, index ^ k, axis, keepdims=False)
        for k in range(values.shape[axis])
    ]


def tree_sum(parts):
    parts = [part.astype(F32) for part in parts]
    while len(parts) > 1:
        parts = [parts[k] + parts[k + 1] for k in range(0, len(parts), 2)]
    return parts[0]


def sum_along(values, axis):
    count = lax.axis_size(axis)
    return tree_sum([values] + [swap(values, axis, k) for k in range(1, count)])


def position():
    return jnp.stack([lax.axis_index(axis) for axis in ("dp",) + SEQ]).astype(jnp.int32)


def place_kernel(store, at_ref, *refs):
    store(at_ref[0], at_ref[1], at_ref[2], refs[:-1], refs[-1])


def place(parts, store, shape, block=None, part_blocks=None):
    steps = 1 if block is None else shape[0]
    block = shape if block is None else block
    part_blocks = [part.shape for part in parts] if part_blocks is None else part_blocks

    def spec(dims):
        return pl.BlockSpec(dims, lambda i, at: (i,) + (0,) * (len(dims) - 1))

    return pl.pallas_call(
        functools.partial(place_kernel, store),
        out_shape=jax.ShapeDtypeStruct(shape, parts[0].dtype),
        grid_spec=pltpu.PrefetchScalarGridSpec(
            num_scalar_prefetch=1,
            grid=(steps,),
            in_specs=[spec(dims) for dims in part_blocks],
            out_specs=spec(block),
        ),
        compiler_params=pltpu.CompilerParams(
            dimension_semantics=("arbitrary",), vmem_limit_bytes=VMEM_LIMIT
        ),
        cost_estimate=pl.CostEstimate(
            flops=0, bytes_accessed=4 * math.prod(shape), transcendentals=0
        ),
        name="place",
    )(position(), *parts)


def join_parts(parts, axis):
    shape = parts[0].shape
    full = shape[:axis] + (len(parts),) + shape[axis:]

    def store(dp_index, chip, core, refs, out):
        for k, ref in enumerate(refs):
            if axis == 0:
                out[dp_index ^ k] = ref[...]
            else:
                for lead in range(shape[0]):
                    where = (lead,) + (slice(None),) * (axis - 1) + (dp_index ^ k,)
                    out[where] = ref[lead]

    return place(parts, store, full)


def join_columns(parts, cut):
    groups = len(parts)
    rows, columns = parts[0].shape
    if cut % 128:
        joined = jnp.zeros((groups, rows, columns // cut, cut), parts[0].dtype)
        for k, part in enumerate(parts):
            part = part.reshape(rows, columns // cut, cut)
            index = lax.axis_index("dp") ^ k
            joined = lax.dynamic_update_index_in_dim(joined, part, index, 0)
        return joined.transpose(1, 2, 0, 3).reshape(rows, columns * groups)

    def store(dp_index, chip, core, refs, out):
        for k, ref in enumerate(refs):
            for s in range(columns // cut):
                start = pl.multiple_of((s * groups + (dp_index ^ k)) * cut, 128)
                out[:, pl.ds(start, cut)] = ref[:, s * cut : (s + 1) * cut]

    return place(parts, store, (rows, columns * groups))


def own_part(values, axis):
    return lax.dynamic_index_in_dim(values, lax.axis_index("dp"), axis, keepdims=False)


def fetch_columns(own):
    half = own.shape[1] // 2
    mine = lax.dynamic_slice_in_dim(own, lax.axis_index("core") * half, half, 1)
    return [swap(mine, "dp", k) for k in range(1, lax.axis_size("dp"))]


def share_columns(parts):
    return [swap(part, "core", 1) for part in parts]


def join_rows(parts):
    def store(dp_index, chip, core, refs, out):
        for k, ref in enumerate(refs):
            for flip in range(2):
                out[(chip ^ k) * 2 + (core ^ flip)] = ref[flip]

    return place(parts, store, (2 * len(parts),) + parts[0].shape[1:])


def join_fetched(parts):
    count, model, cut = parts[0].shape
    half = model // 2
    others = (len(parts) - 1) // 2

    def store(dp_index, chip, core, refs, out):
        out[0, :, pl.ds(pl.multiple_of(dp_index * cut, 128), cut)] = refs[0][0]
        for flip in range(2):
            rows = pl.ds(pl.multiple_of((core ^ flip) * half, 128), half)
            for k in range(1, others + 1):
                columns = pl.ds(pl.multiple_of((dp_index ^ k) * cut, 128), cut)
                out[0, rows, columns] = refs[flip * others + k][0]

    blocks = [(1,) + part.shape[1:] for part in parts]
    return place(parts, store, (count, model, model), (1, model, model), blocks)


def after(values, marker):
    return lax.optimization_barrier((values, marker))[0]


def meet(*values):
    return lax.optimization_barrier(values)


def take_columns_kernel(at_ref, in_ref, out_ref):
    out_ref[...] = in_ref[...].astype(BF16)


def take_columns(weights, shards, groups, cut):
    rows = weights.shape[0]
    if cut % 128:
        cut_up = own_part(weights.reshape(rows, shards, groups, cut), 2)
        return cut_up.reshape(rows, shards * cut).astype(BF16)
    return pl.pallas_call(
        take_columns_kernel,
        out_shape=jax.ShapeDtypeStruct((rows, shards * cut), BF16),
        grid_spec=pltpu.PrefetchScalarGridSpec(
            num_scalar_prefetch=1,
            grid=(shards,),
            in_specs=[pl.BlockSpec((rows, cut), lambda s, at: (0, s * groups + at[0]))],
            out_specs=pl.BlockSpec((rows, cut), lambda s, at: (0, s)),
        ),
        cost_estimate=pl.CostEstimate(
            flops=0, bytes_accessed=6 * rows * shards * cut, transcendentals=0
        ),
        name="take_columns",
    )(lax.axis_index("dp").astype(jnp.int32)[None], weights)


def clip_units(grad):
    mean_sq = jnp.mean(grad * grad, axis=-1, keepdims=True)
    return grad * jnp.minimum(1.0, CLIP_RMS * lax.rsqrt(mean_sq + CLIP_EPS))


def adam_update(weight, grad_sum, first_moment, second_moment):
    clipped = clip_units(grad_sum)
    first_new = BETA_ONE * first_moment + (1.0 - BETA_ONE) * clipped
    second_new = BETA_TWO * second_moment + (1.0 - BETA_TWO) * clipped * clipped
    step_size = first_new / CORRECT_ONE / (jnp.sqrt(second_new / CORRECT_TWO) + ADAM_EPS)
    return (first_new, second_new, -RATE * (step_size + DECAY * weight))


def adam_kernel(scale, g_ref, w_ref, m1_ref, m2_ref, g_out, m1_out, m2_out, change_out):
    grad = g_ref[...].astype(F32) * scale
    g_out[...] = grad
    m1_out[...], m2_out[...], change_out[...] = adam_update(
        w_ref[...], grad, m1_ref[...], m2_ref[...]
    )


def adam_call(grad, scale, weight, first, second):
    shape = weight.shape
    columns = shape[-1]
    rows = math.prod(shape[:-1])
    step = min(rows, 262144 // columns)
    spec = pl.BlockSpec((step, columns), lambda i: (i, 0))
    flat = jax.ShapeDtypeStruct((rows, columns), F32)
    outs = pl.pallas_call(
        functools.partial(adam_kernel, scale),
        out_shape=(flat,) * 4,
        grid=(rows // step,),
        in_specs=[spec] * 4,
        out_specs=(spec,) * 4,
        compiler_params=pltpu.CompilerParams(
            dimension_semantics=("arbitrary",), vmem_limit_bytes=VMEM_LIMIT
        ),
        cost_estimate=pl.CostEstimate(
            flops=20 * rows * columns, bytes_accessed=30 * rows * columns, transcendentals=0
        ),
        name="adam",
    )(*[array.reshape(rows, columns) for array in (grad, weight, first, second)])
    return [array.reshape(shape) for array in outs]


def gelu_both(values_in):
    root = math.sqrt(2.0 / math.pi)
    square = values_in * values_in
    bent = jnp.tanh(root * (values_in + 0.044715 * values_in * square))
    half = 0.5 * (1.0 + bent)
    slope = half + 0.5 * values_in * (1.0 - bent * bent) * root * (1.0 + 3.0 * 0.044715 * square)
    return values_in * half, slope.astype(BF16)


def on_device(
    hidden,
    encoder,
    piece_starts,
    grad_out,
    attn_in,
    attn_out,
    ffn_in,
    ffn_out,
    norms,
    first_attn_in,
    first_attn_out,
    first_ffn_in,
    first_ffn_out,
    first_norms,
    second_attn_in,
    second_attn_out,
    second_ffn_in,
    second_ffn_out,
    second_norms,
):
    groups = lax.axis_size("dp")
    shards = lax.axis_size("chip") * lax.axis_size("core")
    rows, model = hidden.shape
    tokens = rows * shards
    width = model // shards
    shard_rows = attn_in.shape[1]
    part_rows = shard_rows // groups
    hidden_units = ffn_in.shape[1]
    unit_cut = hidden_units // (shards * groups)
    block = min(512, tokens)

    core = lax.axis_index("core")
    chips = shards // 2
    gains = lax.optimization_barrier(norms.astype(BF16)).astype(F32)
    resid_in = hidden.astype(F32)
    normed_one, norm_one_back = jax.vjp(layer_norm, resid_in, gains[0], gains[1])
    normed_one = normed_one.astype(BF16)
    normed_all = lax.all_gather(normed_one, SEQ, axis=0, tiled=True)

    to_heads = own_part(attn_in[:3].reshape(3, groups, part_rows, shards, width), 1).astype(BF16)
    to_heads = to_heads.transpose(2, 1, 0, 3).reshape(shards, part_rows, 3 * width)
    to_heads = lax.all_to_all(to_heads, SEQ, split_axis=0, concat_axis=0, tiled=True)
    to_heads = dp_gather(to_heads)
    grad_parts = dp_gather(grad_out)

    def column_part(weights):
        cut = weights.reshape(weights.shape[0], shard_rows, groups, model // groups)
        return own_part(cut, 2).astype(BF16)

    enc_rows = encoder.shape[0]
    keyed = jnp.concatenate(
        [
            column_part(attn_in[4:]),
            encoder.reshape(enc_rows, groups, model // groups).transpose(1, 0, 2),
        ],
        axis=0,
    )
    outer = column_part(jnp.concatenate([attn_out[:1], attn_in[3:4], attn_out[1:]], axis=0))
    up = take_columns(ffn_in, shards, groups, unit_cut)
    down = own_part(ffn_out.reshape(groups, unit_cut, model), 0).astype(BF16)
    to_heads = join_parts(to_heads, 1).reshape(model, 3 * width)
    normed_all, to_heads, grad_parts, keyed, outer, up, down = meet(
        normed_all, to_heads, grad_parts, keyed, outer, up, down
    )

    outer = lax.all_gather(outer, SEQ, axis=1, tiled=True)
    qkv = dot_f32(normed_all, to_heads).astype(BF16)
    keyed = lax.all_gather(after(keyed, qkv), SEQ, axis=1, tiled=True)
    query, key, value = [qkv[:, i * width : (i + 1) * width] for i in range(3)]
    out_heads, self_lse = self_forward(piece_starts, query, key, value, block)
    w_up = lax.all_gather(after(up, out_heads), SEQ, axis=0, tiled=True)
    attended = lax.all_to_all(
        out_heads.reshape(shards, rows, width), SEQ, split_axis=0, concat_axis=0, tiled=True
    )
    outer = after(outer, out_heads)
    outer_parts = fetch_columns(outer[:2])
    attended, outer_parts = meet(attended, outer_parts)
    w_down = lax.all_gather(after(down, attended), SEQ, axis=0, tiled=True)
    outer_shared = share_columns(outer_parts)
    cross_parts = fetch_columns(after(outer[2:], attended))
    w_o, w_cq = join_fetched([outer[:2]] + outer_parts + outer_shared)
    attended = attended.transpose(1, 0, 2).reshape(rows, model)
    first_sum = resid_in + dot_f32(attended, w_o)
    first_sum, cross_parts, keyed = meet(first_sum, cross_parts, keyed)

    keyed_parts = fetch_columns(keyed[:2])
    cross_shared = share_columns(cross_parts)
    normed_two, norm_two_back = jax.vjp(layer_norm, first_sum, gains[2], gains[3])
    normed_two = normed_two.astype(BF16)
    cross_queries = dot_f32(normed_two, w_cq).astype(BF16)
    encoder_all = keyed[2:].transpose(1, 0, 2).reshape(enc_rows * shards, model)
    w_co = join_fetched([outer[2:]] + cross_parts + cross_shared)[0]
    cross_queries, encoder_all, w_co, keyed_parts = meet(
        cross_queries, encoder_all, w_co, keyed_parts
    )
    w_ck, w_cv = join_fetched([keyed[:2]] + keyed_parts + share_columns(keyed_parts))
    cross_kv = jnp.stack([dot_f32(encoder_all, w_ck), dot_f32(encoder_all, w_cv)]).astype(BF16)

    crossed, cross_lse = cross_forward(cross_queries, cross_kv)
    second_sum = first_sum + dot_f32(crossed, w_co)

    normed_three, norm_three_back = jax.vjp(layer_norm, second_sum, gains[4], gains[5])
    normed_three = normed_three.astype(BF16)
    ffn_tokens = jnp.concatenate(dp_gather(normed_three), axis=0)
    grad_tokens = jnp.concatenate(grad_parts, axis=0)
    activated, slope = gelu_both(dot_f32(ffn_tokens, w_up))
    activated = activated.astype(BF16)
    grad_down = dot_tn(activated, grad_tokens).astype(BF16)
    activated, slope = after((activated, slope), grad_down)
    grad_down = lax.psum_scatter(grad_down, SEQ, scatter_dimension=0, tiled=True)
    grad_pre = (dot_nt(grad_tokens, w_down) * slope).astype(BF16)
    partial = dot_nt(grad_pre, w_up).astype(BF16)
    grad_three = swap_blocks([partial[k * rows : (k + 1) * rows] for k in range(groups)], "dp")

    activated, grad_pre = after((activated, grad_pre), partial)
    partial = dot_f32(activated, w_down)
    grad_up = dot_tn(ffn_tokens, grad_pre).astype(BF16)
    grad_three, partial, grad_up = meet(grad_three, partial, grad_up)
    grad_up = lax.psum_scatter(grad_up, SEQ, scatter_dimension=0, tiled=True)
    hidden_parts = [partial[:rows]] + [
        partial[k * rows : (k + 1) * rows].astype(BF16) for k in range(1, groups)
    ]

    norm_part, grad_gain_three, grad_shift_three = norm_three_back(tree_sum(grad_three))
    grad_second = grad_out.astype(F32) + norm_part
    grad_cross_branch = grad_second.astype(BF16)
    grad_cross_branch, grad_down = meet(grad_cross_branch, grad_down)
    down_parts = dp_gather(grad_down)
    grad_crossed = dot_nt(grad_cross_branch, w_co).astype(BF16)
    grad_cq, grad_ckv = cross_backward(
        cross_queries, cross_kv, crossed, grad_crossed, cross_lse, width
    )
    grad_cq, down_parts, grad_ckv = meet(grad_cq, down_parts, grad_ckv)
    grad_ckv = lax.psum_scatter(grad_ckv, SEQ, scatter_dimension=0, tiled=True)
    grad_ckv = grad_ckv.reshape(2, enc_rows * shards, width)
    grad_normed_two = dot_nt(grad_cq, w_cq)
    norm_part, grad_gain_two, grad_shift_two = norm_two_back(grad_normed_two)
    grad_first = grad_second + norm_part
    grad_self_branch = grad_first.astype(BF16)
    grad_attended = dot_nt(grad_self_branch, w_o).astype(BF16)
    grad_w_co = dot_tn(crossed, grad_cross_branch)
    grad_w_cq = dot_tn(normed_two, grad_cq)
    grad_w_o = dot_tn(attended, grad_self_branch)
    local = jnp.stack([grad.astype(BF16) for grad in (grad_w_o, grad_w_co, grad_w_cq)])
    local = pick_blocks(local.reshape(3, chips, 2, shard_rows, model), "core", 2)
    grad_attended, local = meet(grad_attended, local)
    grad_heads = lax.all_to_all(
        grad_attended.reshape(rows, shards, width).transpose(1, 0, 2),
        SEQ,
        split_axis=0,
        concat_axis=0,
        tiled=True,
    ).reshape(tokens, width)

    scale = 1.0 / math.sqrt(tokens * groups)
    local = swap_blocks(local, "core")
    whole_down = join_parts(after(down_parts, grad_attended), 0)
    local, whole_down = meet(local, whole_down)
    local = tree_sum(local).astype(BF16).reshape(3, chips, groups, part_rows, model)
    local = pick_blocks(local, "dp", 2)
    sum_down, *upd_down = adam_call(whole_down, scale, ffn_out, first_ffn_out, second_ffn_out)
    grad_heads, local, sum_down, grad_up = meet(grad_heads, local, sum_down, grad_up)

    local = swap_blocks(local, "dp")
    grad_flat = self_backward(
        piece_starts, query, key, value, out_heads, grad_heads, self_lse, block
    )
    grad_flat, local = meet(grad_flat, local)

    def reduce_headed(inputs, grads):
        headed = dot_tn(inputs, grads).astype(BF16)
        return headed.reshape(shards, groups, part_rows, grads.shape[1])

    def headed_rows(headed):
        count = headed[0].shape[2] // width
        headed = join_rows(headed).reshape(shards, part_rows, count, width)
        return headed.transpose(2, 1, 0, 3).reshape(count, part_rows, model)

    partial = dot_nt(grad_flat, to_heads).astype(BF16)
    grad_normed_one = lax.psum_scatter(partial, SEQ, scatter_dimension=0, tiled=True)

    grad_flat, local, grad_up, hidden_parts = after((grad_flat, local, grad_up, hidden_parts), partial)
    up_parts = dp_gather(grad_up)
    self_part = reduce_headed(normed_all, grad_flat)
    local = pick_blocks(tree_sum(local).astype(BF16), "chip", 1)
    grad_ckv, local, self_part = meet(grad_ckv, local, self_part)
    cross_part = reduce_headed(encoder_all, jnp.concatenate([grad_ckv[0], grad_ckv[1]], axis=1))
    headed = jnp.concatenate([self_part, cross_part], axis=3).transpose(1, 0, 2, 3)
    headed = lax.all_to_all(headed, "dp", split_axis=0, concat_axis=0, tiled=True)
    local = swap_blocks(local, "chip")
    seq = lax.axis_index("chip") * 2 + core
    key_columns = lax.dynamic_slice_in_dim(w_ck, seq * width, width, 1)
    value_columns = lax.dynamic_slice_in_dim(w_cv, seq * width, width, 1)
    partial_enc = dot_nt(grad_ckv[0], key_columns) + dot_nt(grad_ckv[1], value_columns)
    partial_enc, up_parts = meet(partial_enc.astype(BF16), up_parts)
    grad_encoder = lax.psum_scatter(partial_enc, SEQ, scatter_dimension=0, tiled=True)
    whole_up = join_columns(up_parts, unit_cut)
    sum_up, *upd_up = adam_call(whole_up, scale, ffn_in, first_ffn_in, second_ffn_in)
    headed, sum_up, local = meet(headed, sum_up, local)

    headed = jnp.sum(headed.astype(F32), axis=0).astype(BF16)
    own, given = pick_blocks(headed.reshape(chips, 2, part_rows, 5 * width), "core", 1)
    given = swap(given, "core", 1)
    local = tree_sum(local).astype(BF16)
    given, own, local = meet(given, own, local)
    hidden_parts = swap_blocks(after(hidden_parts, local), "dp")
    headed = pick_blocks(jnp.stack([own, given], axis=1), "chip", 0)
    headed = swap_blocks(headed, "chip")
    headed, local, hidden_parts = meet(headed, local, hidden_parts)
    local_parts = dp_gather(local)
    out_hidden = second_sum + tree_sum(hidden_parts)
    headed = headed_rows(headed)
    headed, local_parts, out_hidden = meet(headed, local_parts, out_hidden)
    headed_parts = dp_gather(headed)
    local = join_parts(local_parts, 1).reshape(3, shard_rows, model)
    grad_normed_one, local = meet(grad_normed_one, local)
    norm_part, grad_gain_one, grad_shift_one = norm_one_back(grad_normed_one.astype(F32))
    grad_hidden = grad_first + norm_part
    sum_norms = jnp.stack(
        [
            grad_gain_one,
            grad_shift_one,
            grad_gain_two,
            grad_shift_two,
            grad_gain_three,
            grad_shift_three,
        ]
    )
    sum_norms = sum_along(sum_norms * scale, "core")
    sum_norms, headed_parts = meet(sum_norms, headed_parts)
    sum_norms = sum_along(sum_norms, "chip")
    whole_in = join_parts(headed_parts, 1).reshape(5, shard_rows, model)
    whole_in = jnp.concatenate([whole_in[:3], local[2:], whole_in[3:]])
    sum_out, *upd_out = adam_call(local[:2], scale, attn_out, first_attn_out, second_attn_out)
    sum_norms, sum_out, whole_in = meet(sum_norms, sum_out, whole_in)
    norm_total = sum_along(sum_norms, "dp")
    sum_in, *upd_in = adam_call(whole_in, scale, attn_in, first_attn_in, second_attn_in)
    norm_total, sum_in, grad_encoder = meet(norm_total, sum_in, grad_encoder)
    grad_encoder = grad_encoder.astype(F32)
    upd_norms = adam_update(norms, norm_total, first_norms, second_norms)
    return (
        out_hidden,
        grad_hidden,
        grad_encoder,
        sum_in,
        sum_out,
        sum_up,
        sum_down,
        norm_total,
        upd_in[0],
        upd_out[0],
        upd_up[0],
        upd_down[0],
        upd_norms[0],
        upd_in[1],
        upd_out[1],
        upd_up[1],
        upd_down[1],
        upd_norms[1],
        upd_in[2],
        upd_out[2],
        upd_up[2],
        upd_down[2],
        upd_norms[2],
    )


def solution(mesh):
    groups, shards = mesh.shape["dp"], mesh.shape["seq"]
    split = Mesh(mesh.devices.reshape(groups, shards // 2, 2), ("dp",) + SEQ)
    token = P(("dp",) + SEQ, None)
    stacked = P(None, SEQ, None)
    flat = P(SEQ, None)
    params = (stacked, stacked, flat, flat, P())
    return jax.shard_map(
        on_device,
        mesh=split,
        in_specs=(token, token, P("dp", None), token) + params * 3,
        out_specs=(token, token, token) + params * 4,
        check_vma=False,
    )
```

```python
import functools
import math

import jax
import jax.numpy as jnp
from jax import lax
from jax.experimental import pallas as pl
from jax.experimental.pallas import tpu as pltpu
from jax.sharding import Mesh
from jax.sharding import PartitionSpec as P

HEAD_DIM = 64
PIECE_LEN = 256

NORM_EPS = 1e-05
SCALE = 0.125
BETA_ONE = 0.9
BETA_TWO = 0.95
CORRECT_ONE = 1.0 - 0.9**8
CORRECT_TWO = 1.0 - 0.95**8
ADAM_EPS = 1e-08
RATE = 0.01
DECAY = 0.1
CLIP_RMS = 0.05
CLIP_EPS = 1e-06
MASKED = -1e30

SEQ = ("chip", "core")
BF16 = jnp.bfloat16
F32 = jnp.float32
VMEM_LIMIT = 48 * 1024 * 1024
NT = (((1,), (1,)), ((), ()))
TN = (((0,), (0,)), ((), ()))


def layer_norm(values_in, gain, shift):
    mean_val = jnp.mean(values_in, axis=-1, keepdims=True)
    centred = values_in - mean_val
    variance = jnp.mean(centred * centred, axis=-1, keepdims=True)
    return centred * lax.rsqrt(variance + NORM_EPS) * gain + shift


def dot_f32(left, right):
    return jnp.dot(left, right, preferred_element_type=F32)


def dot_nt(left, right):
    return lax.dot_general(left, right, NT, preferred_element_type=F32)


def dot_tn(left, right):
    return lax.dot_general(left, right, TN, preferred_element_type=F32)


def key_limit(positions, starts_ref, pieces):
    limit = positions + 1
    for piece in range(pieces):
        start = starts_ref[0, piece]
        inside = (positions >= start) & (positions < start + PIECE_LEN)
        limit = jnp.where(inside, jnp.maximum(limit, start + PIECE_LEN), limit)
    return limit


def spills_over(boundary, starts_ref, pieces):
    over = jnp.bool_(False)
    for piece in range(pieces):
        start = starts_ref[0, piece]
        over = over | ((start < boundary) & (start + PIECE_LEN > boundary))
    return over


def self_fwd_kernel(heads, pieces, block, starts_ref, q_ref, k_ref, v_ref, o_ref, lse_ref, s_ref):
    step = pl.program_id(0)
    last = pl.num_programs(0) - 1
    row_pos = step * block + lax.broadcasted_iota(jnp.int32, (block, 1), 0)
    limit = key_limit(row_pos, starts_ref, pieces)
    over = spills_over((step + 1) * block, starts_ref, pieces) & (step < last)
    blocks = step + 1 + over.astype(jnp.int32)
    for head in range(heads):
        cols = slice(head * HEAD_DIM, (head + 1) * HEAD_DIM)
        query = q_ref[:, cols] * BF16(SCALE)

        def scores(index):
            rows = pl.ds(pl.multiple_of(index * block, block), block)
            return dot_nt(query, k_ref[rows, cols])

        def masked_scores(index):
            key_pos = index * block + lax.broadcasted_iota(jnp.int32, (1, block), 1)
            return jnp.where(key_pos < limit, scores(index), MASKED)

        def lane_max(peak, values):
            for at in range(0, block, 128):
                peak = jnp.maximum(peak, values[:, at : at + 128])
            return peak

        def first_pass(index, peak):
            values = scores(index)
            s_ref[index] = values
            return lane_max(peak, values)

        def edge_pass(index, peak):
            values = masked_scores(index)
            s_ref[index] = values
            return lane_max(peak, values)

        peak = jnp.full((block, 128), MASKED, F32)
        peak = lax.fori_loop(0, step, first_pass, peak)
        peak = lax.fori_loop(step, blocks, edge_pass, peak)
        peak = jnp.max(peak, axis=1, keepdims=True)

        def second_pass(index, carry):
            total, out = carry
            terms = jnp.exp(s_ref[index] - peak)
            for at in range(0, block, 128):
                total = total + terms[:, at : at + 128]
            rows = pl.ds(pl.multiple_of(index * block, block), block)
            return total, out + dot_f32(terms.astype(BF16), v_ref[rows, cols])

        total, out = lax.fori_loop(
            0,
            blocks,
            second_pass,
            (jnp.zeros((block, 128), F32), jnp.zeros((block, HEAD_DIM), F32)),
        )
        total = jnp.sum(total, axis=1, keepdims=True)
        o_ref[:, cols] = (out / total).astype(BF16)
        lse = jnp.broadcast_to(peak + jnp.log(total), (block, 128))
        lse_ref[head] = jnp.transpose(lse)[:8]


def self_forward(starts, query, key, value, block):
    tokens, width = query.shape
    heads = width // HEAD_DIM
    pieces = starts.shape[1]
    whole = pl.BlockSpec((tokens, width), lambda i, s: (0, 0))
    flops = 2 * 2 * heads * tokens * tokens * HEAD_DIM
    return pl.pallas_call(
        functools.partial(self_fwd_kernel, heads, pieces, block),
        out_shape=(
            jax.ShapeDtypeStruct((tokens, width), BF16),
            jax.ShapeDtypeStruct((heads, 8, tokens), F32),
        ),
        grid_spec=pltpu.PrefetchScalarGridSpec(
            num_scalar_prefetch=1,
            grid=(tokens // block,),
            in_specs=[pl.BlockSpec((block, width), lambda i, s: (i, 0)), whole, whole],
            out_specs=(
                pl.BlockSpec((block, width), lambda i, s: (i, 0)),
                pl.BlockSpec((heads, 8, block), lambda i, s: (0, 0, i)),
            ),
            scratch_shapes=[pltpu.VMEM((tokens // block, block, block), F32)],
        ),
        compiler_params=pltpu.CompilerParams(
            dimension_semantics=("arbitrary",), vmem_limit_bytes=VMEM_LIMIT
        ),
        cost_estimate=pl.CostEstimate(
            flops=flops, bytes_accessed=8 * tokens * width, transcendentals=heads * tokens * tokens
        ),
        name="self_forward",
    )(starts, query, key, value)


def self_bwd_kernel(
    heads,
    pieces,
    block,
    starts_ref,
    q_ref,
    k_ref,
    v_ref,
    o_ref,
    do_ref,
    lse_ref,
    flat_ref,
    dk_acc,
    dv_acc,
):
    step = pl.program_id(0)
    last = pl.num_programs(0) - 1
    width = dk_acc.shape[1]

    @pl.when(step == 0)
    def _():
        dk_acc[...] = jnp.zeros_like(dk_acc)
        dv_acc[...] = jnp.zeros_like(dv_acc)

    col_pos = step * block + lax.broadcasted_iota(jnp.int32, (1, block), 1)
    limit = key_limit(col_pos, starts_ref, pieces)
    over = spills_over((step + 1) * block, starts_ref, pieces) & (step < last)
    blocks = step + 1 + over.astype(jnp.int32)
    for head in range(heads):
        cols = slice(head * HEAD_DIM, (head + 1) * HEAD_DIM)
        query = q_ref[:, cols] * BF16(SCALE)
        grad = do_ref[:, cols]
        product = grad.astype(F32) * o_ref[:, cols].astype(F32)
        delta = lax.dot_general(
            jnp.ones((8, HEAD_DIM), F32),
            product,
            NT,
            precision=lax.Precision.HIGHEST,
            preferred_element_type=F32,
        )[:1]
        lse = lse_ref[head][:1]

        def one_block(masked, index, dq):
            rows = pl.ds(pl.multiple_of(index * block, block), block)
            key = k_ref[rows, cols]
            scores = dot_nt(key, query)
            if masked:
                key_pos = index * block + lax.broadcasted_iota(jnp.int32, (block, 1), 0)
                scores = jnp.where(key_pos < limit, scores, MASKED)
            weights = jnp.exp(scores - lse)
            grad_weights = dot_nt(v_ref[rows, cols], grad)
            dv_acc[rows, cols] += dot_f32(weights.astype(BF16), grad)
            grad_scores = (weights * (grad_weights - delta)).astype(BF16)
            dk_acc[rows, cols] += dot_f32(grad_scores, query)
            return dq + dot_tn(grad_scores, key)

        dq = jnp.zeros((block, HEAD_DIM), F32)
        dq = lax.fori_loop(0, step, functools.partial(one_block, False), dq)
        dq = lax.fori_loop(step, blocks, functools.partial(one_block, True), dq)
        dq = (dq * SCALE).astype(BF16)
        flat_ref[pl.ds(pl.multiple_of(step * block, block), block), cols] = dq

    @pl.when(step == last)
    def _():
        for which, acc in ((1, dk_acc), (2, dv_acc)):
            flat_ref[:, which * width : (which + 1) * width] = acc[...].astype(BF16)


def self_backward(starts, query, key, value, out, grad, lse, block):
    tokens, width = query.shape
    heads = width // HEAD_DIM
    pieces = starts.shape[1]
    whole = pl.BlockSpec((tokens, width), lambda i, s: (0, 0))
    rows = pl.BlockSpec((block, width), lambda i, s: (i, 0))
    flops = 5 * 2 * heads * tokens * tokens * HEAD_DIM
    return pl.pallas_call(
        functools.partial(self_bwd_kernel, heads, pieces, block),
        out_shape=jax.ShapeDtypeStruct((tokens, 3 * width), BF16),
        grid_spec=pltpu.PrefetchScalarGridSpec(
            num_scalar_prefetch=1,
            grid=(tokens // block,),
            in_specs=[
                rows,
                whole,
                whole,
                rows,
                rows,
                pl.BlockSpec((heads, 8, block), lambda i, s: (0, 0, i)),
            ],
            out_specs=pl.BlockSpec((tokens, 3 * width), lambda i, s: (0, 0)),
            scratch_shapes=[pltpu.VMEM((tokens, width), F32), pltpu.VMEM((tokens, width), F32)],
        ),
        compiler_params=pltpu.CompilerParams(
            dimension_semantics=("arbitrary",), vmem_limit_bytes=VMEM_LIMIT
        ),
        cost_estimate=pl.CostEstimate(
            flops=flops, bytes_accessed=16 * tokens * width, transcendentals=heads * tokens * tokens
        ),
        name="self_backward",
    )(starts, query, key, value, out, grad, lse)


def cross_fwd_kernel(q_ref, k_ref, v_ref, o_ref, lse_ref):
    rows = q_ref.shape[0]
    for head in range(q_ref.shape[1] // HEAD_DIM):
        cols = slice(head * HEAD_DIM, (head + 1) * HEAD_DIM)
        scores = dot_nt(q_ref[:, cols] * BF16(SCALE), k_ref[:, cols])
        peak = jnp.max(scores, axis=1, keepdims=True)
        terms = jnp.exp(scores - peak)
        total = jnp.sum(terms, axis=1, keepdims=True)
        o_ref[:, cols] = (dot_f32(terms.astype(BF16), v_ref[:, cols]) / total).astype(BF16)
        lse = jnp.broadcast_to(peak + jnp.log(total), (rows, 128))
        lse_ref[head] = jnp.transpose(lse)[:8]


def cross_forward(query, key_value):
    rows, width = query.shape
    keys = key_value.shape[1]
    heads = width // HEAD_DIM
    return pl.pallas_call(
        lambda q, k, v, o, lse: cross_fwd_kernel(q, k, v, o, lse),
        out_shape=(
            jax.ShapeDtypeStruct((rows, width), BF16),
            jax.ShapeDtypeStruct((heads, 8, rows), F32),
        ),
        grid=(width // 128,),
        in_specs=[
            pl.BlockSpec((rows, 128), lambda i: (0, i)),
            pl.BlockSpec((None, keys, 128), lambda i: (0, 0, i)),
            pl.BlockSpec((None, keys, 128), lambda i: (1, 0, i)),
        ],
        out_specs=(
            pl.BlockSpec((rows, 128), lambda i: (0, i)),
            pl.BlockSpec((2, 8, rows), lambda i: (i, 0, 0)),
        ),
        compiler_params=pltpu.CompilerParams(
            dimension_semantics=("arbitrary",), vmem_limit_bytes=VMEM_LIMIT
        ),
        cost_estimate=pl.CostEstimate(
            flops=4 * rows * keys * width,
            bytes_accessed=4 * rows * width + 4 * keys * width,
            transcendentals=heads * rows * keys,
        ),
        name="cross_forward",
    )(query, key_value, key_value)


def cross_bwd_kernel(width, q_ref, k_ref, v_ref, o_ref, do_ref, lse_ref, dq_ref, dkv_ref):
    for head in range(q_ref.shape[1] // HEAD_DIM):
        cols = slice(head * HEAD_DIM, (head + 1) * HEAD_DIM)
        owner = head * HEAD_DIM // width
        own_cols = slice(head * HEAD_DIM % width, head * HEAD_DIM % width + HEAD_DIM)
        query = q_ref[:, cols] * BF16(SCALE)
        grad = do_ref[:, cols]
        product = grad.astype(F32) * o_ref[:, cols].astype(F32)
        delta = lax.dot_general(
            jnp.ones((8, HEAD_DIM), F32),
            product,
            NT,
            precision=lax.Precision.HIGHEST,
            preferred_element_type=F32,
        )[:1]
        key = k_ref[:, cols]
        weights = jnp.exp(dot_nt(key, query) - lse_ref[head][:1])
        grad_weights = dot_nt(v_ref[:, cols], grad)
        dkv_ref[owner, 1, :, own_cols] = dot_f32(weights.astype(BF16), grad).astype(BF16)
        grad_scores = (weights * (grad_weights - delta)).astype(BF16)
        dkv_ref[owner, 0, :, own_cols] = dot_f32(grad_scores, query).astype(BF16)
        dq_ref[:, cols] = (dot_tn(grad_scores, key) * SCALE).astype(BF16)


def cross_backward(query, key_value, out, grad, lse, owner_width):
    rows, width = query.shape
    keys = key_value.shape[1]
    heads = width // HEAD_DIM
    rows_spec = pl.BlockSpec((rows, 128), lambda i: (0, i))
    dkv_block = (128 // owner_width, 2, keys, owner_width)
    return pl.pallas_call(
        functools.partial(cross_bwd_kernel, owner_width),
        out_shape=(
            jax.ShapeDtypeStruct((rows, width), BF16),
            jax.ShapeDtypeStruct((width // owner_width, 2, keys, owner_width), BF16),
        ),
        grid=(width // 128,),
        in_specs=[
            rows_spec,
            pl.BlockSpec((None, keys, 128), lambda i: (0, 0, i)),
            pl.BlockSpec((None, keys, 128), lambda i: (1, 0, i)),
            rows_spec,
            rows_spec,
            pl.BlockSpec((2, 8, rows), lambda i: (i, 0, 0)),
        ],
        out_specs=(rows_spec, pl.BlockSpec(dkv_block, lambda i: (i, 0, 0, 0))),
        compiler_params=pltpu.CompilerParams(
            dimension_semantics=("arbitrary",), vmem_limit_bytes=VMEM_LIMIT
        ),
        cost_estimate=pl.CostEstimate(
            flops=10 * rows * keys * width,
            bytes_accessed=8 * rows * width + 8 * keys * width,
            transcendentals=heads * rows * keys,
        ),
        name="cross_backward",
    )(query, key_value, key_value, out, grad, lse)


def swap(values, axis, offset):
    count = lax.axis_size(axis)
    return lax.ppermute(values, axis, [(index, index ^ offset) for index in range(count)])


def dp_gather(values):
    return [values] + [swap(values, "dp", k) for k in range(1, lax.axis_size("dp"))]


def swap_blocks(blocks, axis):
    return [blocks[0]] + [swap(blocks[k], axis, k) for k in range(1, len(blocks))]


def pick_blocks(values, axis_name, axis):
    index = lax.axis_index(axis_name)
    return [
        lax.dynamic_index_in_dim(values, index ^ k, axis, keepdims=False)
        for k in range(values.shape[axis])
    ]


def tree_sum(parts):
    parts = [part.astype(F32) for part in parts]
    while len(parts) > 1:
        parts = [parts[k] + parts[k + 1] for k in range(0, len(parts), 2)]
    return parts[0]


def sum_along(values, axis):
    count = lax.axis_size(axis)
    return tree_sum([values] + [swap(values, axis, k) for k in range(1, count)])


def position():
    return jnp.stack([lax.axis_index(axis) for axis in ("dp",) + SEQ]).astype(jnp.int32)


def place_kernel(store, at_ref, *refs):
    store(at_ref[0], at_ref[1], at_ref[2], refs[:-1], refs[-1])


def place(parts, store, shape, block=None, part_blocks=None):
    steps = 1 if block is None else shape[0]
    block = shape if block is None else block
    part_blocks = [part.shape for part in parts] if part_blocks is None else part_blocks

    def spec(dims):
        return pl.BlockSpec(dims, lambda i, at: (i,) + (0,) * (len(dims) - 1))

    return pl.pallas_call(
        functools.partial(place_kernel, store),
        out_shape=jax.ShapeDtypeStruct(shape, parts[0].dtype),
        grid_spec=pltpu.PrefetchScalarGridSpec(
            num_scalar_prefetch=1,
            grid=(steps,),
            in_specs=[spec(dims) for dims in part_blocks],
            out_specs=spec(block),
        ),
        compiler_params=pltpu.CompilerParams(
            dimension_semantics=("arbitrary",), vmem_limit_bytes=VMEM_LIMIT
        ),
        cost_estimate=pl.CostEstimate(
            flops=0, bytes_accessed=4 * math.prod(shape), transcendentals=0
        ),
        name="place",
    )(position(), *parts)


def join_parts(parts, axis):
    shape = parts[0].shape
    full = shape[:axis] + (len(parts),) + shape[axis:]

    def store(dp_index, chip, core, refs, out):
        for k, ref in enumerate(refs):
            if axis == 0:
                out[dp_index ^ k] = ref[...]
            else:
                for lead in range(shape[0]):
                    where = (lead,) + (slice(None),) * (axis - 1) + (dp_index ^ k,)
                    out[where] = ref[lead]

    return place(parts, store, full)


def own_part(values, axis):
    return lax.dynamic_index_in_dim(values, lax.axis_index("dp"), axis, keepdims=False)


def fetch_columns(own):
    half = own.shape[1] // 2
    mine = lax.dynamic_slice_in_dim(own, lax.axis_index("core") * half, half, 1)
    return [swap(mine, "dp", k) for k in range(1, lax.axis_size("dp"))]


def share_columns(parts):
    return [swap(part, "core", 1) for part in parts]


def join_rows(parts):
    def store(dp_index, chip, core, refs, out):
        for k, ref in enumerate(refs):
            for flip in range(2):
                out[(chip ^ k) * 2 + (core ^ flip)] = ref[flip]

    return place(parts, store, (2 * len(parts),) + parts[0].shape[1:])


def join_fetched(parts):
    count, model, cut = parts[0].shape
    half = model // 2
    others = (len(parts) - 1) // 2

    def store(dp_index, chip, core, refs, out):
        out[0, :, pl.ds(pl.multiple_of(dp_index * cut, 128), cut)] = refs[0][0]
        for flip in range(2):
            rows = pl.ds(pl.multiple_of((core ^ flip) * half, 128), half)
            for k in range(1, others + 1):
                columns = pl.ds(pl.multiple_of((dp_index ^ k) * cut, 128), cut)
                out[0, rows, columns] = refs[flip * others + k][0]

    blocks = [(1,) + part.shape[1:] for part in parts]
    return place(parts, store, (count, model, model), (1, model, model), blocks)


def after(values, marker):
    return lax.optimization_barrier((values, marker))[0]


def meet(*values):
    return lax.optimization_barrier(values)


def take_columns_kernel(at_ref, in_ref, out_ref):
    out_ref[...] = in_ref[...].astype(BF16)


def take_columns(weights, shards, groups, cut):
    rows = weights.shape[0]
    if cut % 128:
        cut_up = own_part(weights.reshape(rows, shards, groups, cut), 2)
        return cut_up.reshape(rows, shards * cut).astype(BF16)
    return pl.pallas_call(
        take_columns_kernel,
        out_shape=jax.ShapeDtypeStruct((rows, shards * cut), BF16),
        grid_spec=pltpu.PrefetchScalarGridSpec(
            num_scalar_prefetch=1,
            grid=(shards,),
            in_specs=[pl.BlockSpec((rows, cut), lambda s, at: (0, s * groups + at[0]))],
            out_specs=pl.BlockSpec((rows, cut), lambda s, at: (0, s)),
        ),
        cost_estimate=pl.CostEstimate(
            flops=0, bytes_accessed=6 * rows * shards * cut, transcendentals=0
        ),
        name="take_columns",
    )(lax.axis_index("dp").astype(jnp.int32)[None], weights)


def encoder_partial_kernel(at_ref, grad_ref, key_ref, value_ref, out_ref):
    total = dot_nt(grad_ref[0], key_ref[...]) + dot_nt(grad_ref[1], value_ref[...])
    out_ref[...] = total.astype(BF16)


def encoder_partial(grad, w_keyed):
    rows, width = grad.shape[1:]
    model = w_keyed.shape[1]
    seq = lax.axis_index("chip") * lax.axis_size("core") + lax.axis_index("core")
    if width % 128:
        own = lax.dynamic_slice_in_dim(w_keyed, seq * width, width, 2)
        return (dot_nt(grad[0], own[0]) + dot_nt(grad[1], own[1])).astype(BF16)
    step = min(rows, 256)
    return pl.pallas_call(
        encoder_partial_kernel,
        out_shape=jax.ShapeDtypeStruct((rows, model), BF16),
        grid_spec=pltpu.PrefetchScalarGridSpec(
            num_scalar_prefetch=1,
            grid=(rows // step,),
            in_specs=[
                pl.BlockSpec((2, step, width), lambda i, at: (0, i, 0)),
                pl.BlockSpec((None, model, width), lambda i, at: (0, 0, at[0])),
                pl.BlockSpec((None, model, width), lambda i, at: (1, 0, at[0])),
            ],
            out_specs=pl.BlockSpec((step, model), lambda i, at: (i, 0)),
        ),
        compiler_params=pltpu.CompilerParams(
            dimension_semantics=("arbitrary",), vmem_limit_bytes=VMEM_LIMIT
        ),
        cost_estimate=pl.CostEstimate(
            flops=4 * rows * model * width, bytes_accessed=4 * rows * model, transcendentals=0
        ),
        name="encoder_partial",
    )(seq.astype(jnp.int32)[None], grad, w_keyed, w_keyed)


def join_natural_kernel(cut, in_ref, out_ref):
    groups = in_ref.shape[0]
    for index in range(groups):
        for s in range(in_ref.shape[2] // cut):
            start = (s * groups + index) * cut
            out_ref[:, start : start + cut] = in_ref[index, :, s * cut : (s + 1) * cut]


def join_natural(stacked, cut):
    groups, rows, columns = stacked.shape
    return pl.pallas_call(
        functools.partial(join_natural_kernel, cut),
        out_shape=jax.ShapeDtypeStruct((rows, columns * groups), stacked.dtype),
        compiler_params=pltpu.CompilerParams(vmem_limit_bytes=VMEM_LIMIT),
        cost_estimate=pl.CostEstimate(
            flops=0, bytes_accessed=4 * rows * columns * groups, transcendentals=0
        ),
        name="join_natural",
    )(stacked)


def dp_stack(values):
    copies = jnp.broadcast_to(values[None], (lax.axis_size("dp"),) + values.shape)
    return lax.all_to_all(copies, "dp", split_axis=0, concat_axis=0, tiled=True)


def clip_units(grad):
    mean_sq = jnp.mean(grad * grad, axis=-1, keepdims=True)
    return grad * jnp.minimum(1.0, CLIP_RMS * lax.rsqrt(mean_sq + CLIP_EPS))


def adam_update(weight, grad_sum, first_moment, second_moment):
    clipped = clip_units(grad_sum)
    first_new = BETA_ONE * first_moment + (1.0 - BETA_ONE) * clipped
    second_new = BETA_TWO * second_moment + (1.0 - BETA_TWO) * clipped * clipped
    step_size = first_new / CORRECT_ONE / (jnp.sqrt(second_new / CORRECT_TWO) + ADAM_EPS)
    return (first_new, second_new, -RATE * (step_size + DECAY * weight))


def adam_kernel(scale, g_ref, w_ref, m1_ref, m2_ref, g_out, m1_out, m2_out, change_out):
    grad = g_ref[...].astype(F32) * scale
    g_out[...] = grad
    m1_out[...], m2_out[...], change_out[...] = adam_update(
        w_ref[...], grad, m1_ref[...], m2_ref[...]
    )


def adam_call(grad, scale, weight, first, second):
    shape = weight.shape
    columns = shape[-1]
    rows = math.prod(shape[:-1])
    step = min(rows, 262144 // columns)
    spec = pl.BlockSpec((step, columns), lambda i: (i, 0))
    flat = jax.ShapeDtypeStruct((rows, columns), F32)
    outs = pl.pallas_call(
        functools.partial(adam_kernel, scale),
        out_shape=(flat,) * 4,
        grid=(rows // step,),
        in_specs=[spec] * 4,
        out_specs=(spec,) * 4,
        compiler_params=pltpu.CompilerParams(
            dimension_semantics=("arbitrary",), vmem_limit_bytes=VMEM_LIMIT
        ),
        cost_estimate=pl.CostEstimate(
            flops=20 * rows * columns, bytes_accessed=30 * rows * columns, transcendentals=0
        ),
        name="adam",
    )(*[array.reshape(rows, columns) for array in (grad, weight, first, second)])
    return [array.reshape(shape) for array in outs]


def gelu_both(values_in):
    root = math.sqrt(2.0 / math.pi)
    square = values_in * values_in
    bent = jnp.tanh(root * (values_in + 0.044715 * values_in * square))
    half = 0.5 * (1.0 + bent)
    slope = half + 0.5 * values_in * (1.0 - bent * bent) * root * (1.0 + 3.0 * 0.044715 * square)
    return values_in * half, slope.astype(BF16)


def on_device(
    hidden,
    encoder,
    piece_starts,
    grad_out,
    attn_in,
    attn_out,
    ffn_in,
    ffn_out,
    norms,
    first_attn_in,
    first_attn_out,
    first_ffn_in,
    first_ffn_out,
    first_norms,
    second_attn_in,
    second_attn_out,
    second_ffn_in,
    second_ffn_out,
    second_norms,
):
    groups = lax.axis_size("dp")
    shards = lax.axis_size("chip") * lax.axis_size("core")
    rows, model = hidden.shape
    tokens = rows * shards
    width = model // shards
    shard_rows = attn_in.shape[1]
    part_rows = shard_rows // groups
    hidden_units = ffn_in.shape[1]
    unit_cut = hidden_units // (shards * groups)
    block = min(512, tokens)

    core = lax.axis_index("core")
    chips = shards // 2
    gains = lax.optimization_barrier(norms.astype(BF16)).astype(F32)
    resid_in = hidden.astype(F32)
    normed_one, norm_one_back = jax.vjp(layer_norm, resid_in, gains[0], gains[1])
    normed_one = normed_one.astype(BF16)
    normed_all = lax.all_gather(normed_one, SEQ, axis=0, tiled=True)

    to_heads = own_part(attn_in[:3].reshape(3, groups, part_rows, shards, width), 1).astype(BF16)
    to_heads = to_heads.transpose(2, 1, 0, 3).reshape(shards, part_rows, 3 * width)
    to_heads = lax.all_to_all(to_heads, SEQ, split_axis=0, concat_axis=0, tiled=True)
    to_heads = dp_gather(to_heads)
    grad_parts = dp_gather(grad_out)

    def column_part(weights):
        cut = weights.reshape(weights.shape[0], shard_rows, groups, model // groups)
        return own_part(cut, 2).astype(BF16)

    enc_rows = encoder.shape[0]
    keyed = jnp.concatenate(
        [
            column_part(attn_in[4:]),
            encoder.reshape(enc_rows, groups, model // groups).transpose(1, 0, 2),
        ],
        axis=0,
    )
    outer = column_part(jnp.concatenate([attn_out[:1], attn_in[3:4], attn_out[1:]], axis=0))
    up = take_columns(ffn_in, shards, groups, unit_cut)
    down = own_part(ffn_out.reshape(groups, unit_cut, model), 0).astype(BF16)
    to_heads = join_parts(to_heads, 1).reshape(model, 3 * width)
    grad_tokens = jnp.concatenate(grad_parts, axis=0)
    normed_all, to_heads, grad_tokens, keyed, outer, up, down = meet(
        normed_all, to_heads, grad_tokens, keyed, outer, up, down
    )

    outer = lax.all_gather(outer, SEQ, axis=1, tiled=True)
    qkv = dot_f32(normed_all, to_heads).astype(BF16)
    keyed = lax.all_gather(after(keyed, qkv), SEQ, axis=1, tiled=True)
    query, key, value = [qkv[:, i * width : (i + 1) * width] for i in range(3)]
    out_heads, self_lse = self_forward(piece_starts, query, key, value, block)
    w_up = lax.all_gather(after(up, out_heads), SEQ, axis=0, tiled=True)
    attended = lax.all_to_all(
        out_heads.reshape(shards, rows, width), SEQ, split_axis=0, concat_axis=0, tiled=True
    )
    outer = after(outer, out_heads)
    outer_parts = fetch_columns(outer[:2])
    attended, outer_parts = meet(attended, outer_parts)
    w_down = lax.all_gather(after(down, attended), SEQ, axis=0, tiled=True)
    outer_shared = share_columns(outer_parts)
    w_o, w_cq = join_fetched([outer[:2]] + outer_parts + outer_shared)
    attended = attended.transpose(1, 0, 2).reshape(rows, model)
    first_sum = resid_in + dot_f32(attended, w_o)
    first_sum, keyed = meet(first_sum, keyed)

    keyed_parts = fetch_columns(keyed[:2])
    normed_two, norm_two_back = jax.vjp(layer_norm, first_sum, gains[2], gains[3])
    normed_two = normed_two.astype(BF16)
    cross_queries = dot_f32(normed_two, w_cq).astype(BF16)
    encoder_all = keyed[2:].transpose(1, 0, 2).reshape(enc_rows * shards, model)
    cross_queries, encoder_all, keyed_parts = meet(cross_queries, encoder_all, keyed_parts)
    w_keyed = join_fetched([keyed[:2]] + keyed_parts + share_columns(keyed_parts))
    cross_kv = jnp.stack([dot_f32(encoder_all, w_keyed[i]) for i in range(2)]).astype(BF16)

    cross_parts = fetch_columns(after(outer[2:], cross_kv))
    crossed, cross_lse = cross_forward(cross_queries, cross_kv)
    crossed, cross_parts = meet(crossed, cross_parts)
    w_co = join_fetched([outer[2:]] + cross_parts + share_columns(cross_parts))[0]
    second_sum = first_sum + dot_f32(crossed, w_co)

    normed_three, norm_three_back = jax.vjp(layer_norm, second_sum, gains[4], gains[5])
    normed_three = normed_three.astype(BF16)
    ffn_tokens = jnp.concatenate(dp_gather(normed_three), axis=0)
    activated, slope = gelu_both(dot_f32(ffn_tokens, w_up))
    activated = activated.astype(BF16)
    grad_down = dot_tn(activated, grad_tokens).astype(BF16)
    activated, slope = after((activated, slope), grad_down)
    grad_down = lax.psum_scatter(grad_down, SEQ, scatter_dimension=0, tiled=True)
    grad_pre = (dot_nt(grad_tokens, w_down) * slope).astype(BF16)
    partial = dot_nt(grad_pre, w_up).astype(BF16)
    grad_three = swap_blocks([partial[k * rows : (k + 1) * rows] for k in range(groups)], "dp")

    activated, grad_pre = after((activated, grad_pre), partial)
    partial = dot_f32(activated, w_down)
    grad_up = dot_tn(ffn_tokens, grad_pre).astype(BF16)
    grad_three, layer_out, grad_up = meet(grad_three, partial.astype(BF16), grad_up)
    grad_up = lax.psum_scatter(grad_up, SEQ, scatter_dimension=0, tiled=True)
    norm_part, grad_gain_three, grad_shift_three = norm_three_back(tree_sum(grad_three))
    grad_second = grad_out.astype(F32) + norm_part
    grad_cross_branch = grad_second.astype(BF16)
    grad_cross_branch, grad_down = meet(grad_cross_branch, grad_down)
    down_parts = dp_gather(grad_down)
    grad_crossed = dot_nt(grad_cross_branch, w_co).astype(BF16)
    grad_cq, grad_ckv = cross_backward(
        cross_queries, cross_kv, crossed, grad_crossed, cross_lse, width
    )
    grad_cq, down_parts, grad_ckv, layer_out = meet(grad_cq, down_parts, grad_ckv, layer_out)
    hidden_parts = [layer_out[k * rows : (k + 1) * rows] for k in range(groups)]
    early_parts = swap_blocks(hidden_parts[:3], "dp")
    grad_ckv = lax.psum_scatter(grad_ckv, SEQ, scatter_dimension=0, tiled=True)
    grad_ckv = grad_ckv.reshape(2, enc_rows * shards, width)
    grad_normed_two = dot_nt(grad_cq, w_cq)
    norm_part, grad_gain_two, grad_shift_two = norm_two_back(grad_normed_two)
    grad_first = grad_second + norm_part
    grad_self_branch = grad_first.astype(BF16)
    grad_attended = dot_nt(grad_self_branch, w_o).astype(BF16)
    grad_w_co = dot_tn(crossed, grad_cross_branch)
    grad_w_cq = dot_tn(normed_two, grad_cq)
    grad_w_o = dot_tn(attended, grad_self_branch)
    local = jnp.stack([grad.astype(BF16) for grad in (grad_w_o, grad_w_co, grad_w_cq)])
    local = pick_blocks(local.reshape(3, chips, 2, shard_rows, model), "core", 2)
    grad_attended, local, early_parts = meet(grad_attended, local, early_parts)
    grad_heads = lax.all_to_all(
        grad_attended.reshape(rows, shards, width).transpose(1, 0, 2),
        SEQ,
        split_axis=0,
        concat_axis=0,
        tiled=True,
    ).reshape(tokens, width)

    scale = 1.0 / math.sqrt(tokens * groups)
    local = swap_blocks(local, "core")
    whole_down = join_parts(after(down_parts, grad_attended), 0)
    local, whole_down = meet(local, whole_down)
    local = tree_sum(local).astype(BF16).reshape(3, chips, groups, part_rows, model)
    local = pick_blocks(local, "dp", 2)
    local, whole_down = meet(local, whole_down)
    local = swap_blocks(local, "dp")
    sum_down, *upd_down = adam_call(whole_down, scale, ffn_out, first_ffn_out, second_ffn_out)
    grad_heads, local[1], sum_down, grad_up = meet(grad_heads, local[1], sum_down, grad_up)

    grad_flat = self_backward(
        piece_starts, query, key, value, out_heads, grad_heads, self_lse, block
    )
    grad_flat, local = meet(grad_flat, local)

    def reduce_headed(inputs, grads):
        headed = dot_tn(inputs, grads).astype(BF16)
        return headed.reshape(shards, groups, part_rows, grads.shape[1])

    def headed_rows(headed):
        count = headed[0].shape[2] // width
        headed = join_rows(headed).reshape(shards, part_rows, count, width)
        return headed.transpose(2, 1, 0, 3).reshape(count, part_rows, model)

    partial = dot_nt(grad_flat, to_heads).astype(BF16)
    grad_normed_one = lax.psum_scatter(partial, SEQ, scatter_dimension=0, tiled=True)

    grad_flat, local, grad_up, hidden_parts = after((grad_flat, local, grad_up, hidden_parts), partial)
    late_parts = [swap(hidden_parts[k], "dp", k) for k in range(3, groups)]
    self_part = reduce_headed(normed_all, grad_flat)
    local = pick_blocks(tree_sum(local).astype(BF16), "chip", 1)
    grad_ckv, local, self_part, late_parts = meet(grad_ckv, local, self_part, late_parts)
    cross_part = reduce_headed(encoder_all, jnp.concatenate([grad_ckv[0], grad_ckv[1]], axis=1))
    headed = jnp.concatenate([self_part, cross_part], axis=3).transpose(1, 0, 2, 3)
    headed = lax.all_to_all(headed, "dp", split_axis=0, concat_axis=0, tiled=True)
    local = swap_blocks(local, "chip")
    partial_enc = encoder_partial(grad_ckv, w_keyed)
    out_hidden = second_sum + tree_sum(early_parts + late_parts)
    headed, partial_enc, local[:3], out_hidden = meet(headed, partial_enc, local[:3], out_hidden)

    whole_up = dp_stack(after(grad_up, headed))
    headed = jnp.sum(headed.astype(F32), axis=0).astype(BF16)
    own, given = pick_blocks(headed.reshape(chips, 2, part_rows, 5 * width), "core", 1)
    given = swap(given, "core", 1)
    given, own = meet(given, own)
    headed = pick_blocks(jnp.stack([own, given], axis=1), "chip", 0)
    headed = swap_blocks(headed, "chip")
    headed, local, whole_up, partial_enc = meet(headed, local, whole_up, partial_enc)
    grad_encoder = lax.psum_scatter(partial_enc, SEQ, scatter_dimension=0, tiled=True)
    local = tree_sum(local).astype(BF16)
    headed = headed_rows(headed)
    attn_parts = jnp.concatenate([headed[:3], local[2:], headed[3:], local[:2]])
    attn_parts = dp_gather(attn_parts)
    if unit_cut % 128:
        whole_up = whole_up.reshape(groups, shard_rows, shards, unit_cut).transpose(1, 2, 0, 3)
        whole_up = whole_up.reshape(shard_rows, hidden_units)
    else:
        whole_up = join_natural(whole_up, unit_cut)
    sum_up, *upd_up = adam_call(whole_up, scale, ffn_in, first_ffn_in, second_ffn_in)
    grad_normed_one, attn_parts, sum_up = meet(grad_normed_one, attn_parts, sum_up)
    norm_part, grad_gain_one, grad_shift_one = norm_one_back(grad_normed_one.astype(F32))
    grad_hidden = grad_first + norm_part
    sum_norms = jnp.stack(
        [
            grad_gain_one,
            grad_shift_one,
            grad_gain_two,
            grad_shift_two,
            grad_gain_three,
            grad_shift_three,
        ]
    )
    sum_norms = sum_along(sum_norms * scale, "core")
    whole_attn = join_parts(attn_parts, 1).reshape(8, shard_rows, model)
    sum_norms, whole_attn = meet(sum_norms, whole_attn)
    sum_norms = sum_along(sum_norms, "chip")
    sum_in, *upd_in = adam_call(whole_attn[:6], scale, attn_in, first_attn_in, second_attn_in)
    sum_norms, sum_in, grad_encoder = meet(sum_norms, sum_in, grad_encoder)
    norm_total = sum_along(sum_norms, "dp")
    sum_out, *upd_out = adam_call(whole_attn[6:], scale, attn_out, first_attn_out, second_attn_out)
    norm_total, sum_out = meet(norm_total, sum_out)
    grad_encoder = grad_encoder.astype(F32)
    upd_norms = adam_update(norms, norm_total, first_norms, second_norms)
    return (
        out_hidden,
        grad_hidden,
        grad_encoder,
        sum_in,
        sum_out,
        sum_up,
        sum_down,
        norm_total,
        upd_in[0],
        upd_out[0],
        upd_up[0],
        upd_down[0],
        upd_norms[0],
        upd_in[1],
        upd_out[1],
        upd_up[1],
        upd_down[1],
        upd_norms[1],
        upd_in[2],
        upd_out[2],
        upd_up[2],
        upd_down[2],
        upd_norms[2],
    )


def solution(mesh):
    groups, shards = mesh.shape["dp"], mesh.shape["seq"]
    split = Mesh(mesh.devices.reshape(groups, shards // 2, 2), ("dp",) + SEQ)
    token = P(("dp",) + SEQ, None)
    stacked = P(None, SEQ, None)
    flat = P(SEQ, None)
    params = (stacked, stacked, flat, flat, P())
    return jax.shard_map(
        on_device,
        mesh=split,
        in_specs=(token, token, P("dp", None), token) + params * 3,
        out_specs=(token, token, token) + params * 4,
        check_vma=False,
    )
```

```python
import functools
import math

import jax
import jax.numpy as jnp
from jax import lax
from jax.experimental import pallas as pl
from jax.experimental.pallas import tpu as pltpu
from jax.sharding import Mesh
from jax.sharding import PartitionSpec as P

HEAD_DIM = 64
PIECE_LEN = 256

NORM_EPS = 1e-05
SCALE = 0.125
BETA_ONE = 0.9
BETA_TWO = 0.95
CORRECT_ONE = 1.0 - 0.9**8
CORRECT_TWO = 1.0 - 0.95**8
ADAM_EPS = 1e-08
RATE = 0.01
DECAY = 0.1
CLIP_RMS = 0.05
CLIP_EPS = 1e-06
MASKED = -1e30

SEQ = ("chip", "core")
BF16 = jnp.bfloat16
F32 = jnp.float32
VMEM_LIMIT = 48 * 1024 * 1024
NT = (((1,), (1,)), ((), ()))
TN = (((0,), (0,)), ((), ()))


def layer_norm(values_in, gain, shift):
    mean_val = jnp.mean(values_in, axis=-1, keepdims=True)
    centred = values_in - mean_val
    variance = jnp.mean(centred * centred, axis=-1, keepdims=True)
    return centred * lax.rsqrt(variance + NORM_EPS) * gain + shift


def dot_f32(left, right):
    return jnp.dot(left, right, preferred_element_type=F32)


def dot_nt(left, right):
    return lax.dot_general(left, right, NT, preferred_element_type=F32)


def dot_tn(left, right):
    return lax.dot_general(left, right, TN, preferred_element_type=F32)


def key_limit(positions, starts_ref, pieces):
    limit = positions + 1
    for piece in range(pieces):
        start = starts_ref[0, piece]
        inside = (positions >= start) & (positions < start + PIECE_LEN)
        limit = jnp.where(inside, jnp.maximum(limit, start + PIECE_LEN), limit)
    return limit


def spills_over(boundary, starts_ref, pieces):
    over = jnp.bool_(False)
    for piece in range(pieces):
        start = starts_ref[0, piece]
        over = over | ((start < boundary) & (start + PIECE_LEN > boundary))
    return over


def self_fwd_kernel(heads, pieces, block, starts_ref, q_ref, k_ref, v_ref, o_ref, lse_ref, s_ref):
    step = pl.program_id(0)
    last = pl.num_programs(0) - 1
    row_pos = step * block + lax.broadcasted_iota(jnp.int32, (block, 1), 0)
    limit = key_limit(row_pos, starts_ref, pieces)
    over = spills_over((step + 1) * block, starts_ref, pieces) & (step < last)
    blocks = step + 1 + over.astype(jnp.int32)
    for head in range(heads):
        cols = slice(head * HEAD_DIM, (head + 1) * HEAD_DIM)
        query = q_ref[:, cols] * BF16(SCALE)

        def scores(index):
            rows = pl.ds(pl.multiple_of(index * block, block), block)
            return dot_nt(query, k_ref[rows, cols])

        def masked_scores(index):
            key_pos = index * block + lax.broadcasted_iota(jnp.int32, (1, block), 1)
            return jnp.where(key_pos < limit, scores(index), MASKED)

        def lane_max(peak, values):
            for at in range(0, block, 128):
                peak = jnp.maximum(peak, values[:, at : at + 128])
            return peak

        def first_pass(index, peak):
            values = scores(index)
            s_ref[index] = values
            return lane_max(peak, values)

        def edge_pass(index, peak):
            values = masked_scores(index)
            s_ref[index] = values
            return lane_max(peak, values)

        peak = jnp.full((block, 128), MASKED, F32)
        peak = lax.fori_loop(0, step, first_pass, peak)
        peak = lax.fori_loop(step, blocks, edge_pass, peak)
        peak = jnp.max(peak, axis=1, keepdims=True)

        def second_pass(index, carry):
            total, out = carry
            terms = jnp.exp(s_ref[index] - peak)
            for at in range(0, block, 128):
                total = total + terms[:, at : at + 128]
            rows = pl.ds(pl.multiple_of(index * block, block), block)
            return total, out + dot_f32(terms.astype(BF16), v_ref[rows, cols])

        total, out = lax.fori_loop(
            0,
            blocks,
            second_pass,
            (jnp.zeros((block, 128), F32), jnp.zeros((block, HEAD_DIM), F32)),
        )
        total = jnp.sum(total, axis=1, keepdims=True)
        o_ref[:, cols] = (out / total).astype(BF16)
        lse = jnp.broadcast_to(peak + jnp.log(total), (block, 128))
        lse_ref[head] = jnp.transpose(lse)[:8]


def self_forward(starts, query, key, value, block):
    tokens, width = query.shape
    heads = width // HEAD_DIM
    pieces = starts.shape[1]
    whole = pl.BlockSpec((tokens, width), lambda i, s: (0, 0))
    flops = 2 * 2 * heads * tokens * tokens * HEAD_DIM
    return pl.pallas_call(
        functools.partial(self_fwd_kernel, heads, pieces, block),
        out_shape=(
            jax.ShapeDtypeStruct((tokens, width), BF16),
            jax.ShapeDtypeStruct((heads, 8, tokens), F32),
        ),
        grid_spec=pltpu.PrefetchScalarGridSpec(
            num_scalar_prefetch=1,
            grid=(tokens // block,),
            in_specs=[pl.BlockSpec((block, width), lambda i, s: (i, 0)), whole, whole],
            out_specs=(
                pl.BlockSpec((block, width), lambda i, s: (i, 0)),
                pl.BlockSpec((heads, 8, block), lambda i, s: (0, 0, i)),
            ),
            scratch_shapes=[pltpu.VMEM((tokens // block, block, block), F32)],
        ),
        compiler_params=pltpu.CompilerParams(
            dimension_semantics=("arbitrary",), vmem_limit_bytes=VMEM_LIMIT
        ),
        cost_estimate=pl.CostEstimate(
            flops=flops, bytes_accessed=8 * tokens * width, transcendentals=heads * tokens * tokens
        ),
        name="self_forward",
    )(starts, query, key, value)


def self_bwd_kernel(
    heads,
    pieces,
    block,
    starts_ref,
    q_ref,
    k_ref,
    v_ref,
    o_ref,
    do_ref,
    lse_ref,
    flat_ref,
    dk_acc,
    dv_acc,
):
    step = pl.program_id(0)
    last = pl.num_programs(0) - 1
    width = dk_acc.shape[1]

    @pl.when(step == 0)
    def _():
        dk_acc[...] = jnp.zeros_like(dk_acc)
        dv_acc[...] = jnp.zeros_like(dv_acc)

    col_pos = step * block + lax.broadcasted_iota(jnp.int32, (1, block), 1)
    limit = key_limit(col_pos, starts_ref, pieces)
    over = spills_over((step + 1) * block, starts_ref, pieces) & (step < last)
    blocks = step + 1 + over.astype(jnp.int32)
    for head in range(heads):
        cols = slice(head * HEAD_DIM, (head + 1) * HEAD_DIM)
        query = q_ref[:, cols] * BF16(SCALE)
        grad = do_ref[:, cols]
        product = grad.astype(F32) * o_ref[:, cols].astype(F32)
        delta = lax.dot_general(
            jnp.ones((8, HEAD_DIM), F32),
            product,
            NT,
            precision=lax.Precision.HIGHEST,
            preferred_element_type=F32,
        )[:1]
        lse = lse_ref[head][:1]

        def one_block(masked, index, dq):
            rows = pl.ds(pl.multiple_of(index * block, block), block)
            key = k_ref[rows, cols]
            scores = dot_nt(key, query)
            if masked:
                key_pos = index * block + lax.broadcasted_iota(jnp.int32, (block, 1), 0)
                scores = jnp.where(key_pos < limit, scores, MASKED)
            weights = jnp.exp(scores - lse)
            grad_weights = dot_nt(v_ref[rows, cols], grad)
            dv_acc[rows, cols] += dot_f32(weights.astype(BF16), grad)
            grad_scores = (weights * (grad_weights - delta)).astype(BF16)
            dk_acc[rows, cols] += dot_f32(grad_scores, query)
            return dq + dot_tn(grad_scores, key)

        dq = jnp.zeros((block, HEAD_DIM), F32)
        dq = lax.fori_loop(0, step, functools.partial(one_block, False), dq)
        dq = lax.fori_loop(step, blocks, functools.partial(one_block, True), dq)
        dq = (dq * SCALE).astype(BF16)
        flat_ref[pl.ds(pl.multiple_of(step * block, block), block), cols] = dq

    @pl.when(step == last)
    def _():
        for which, acc in ((1, dk_acc), (2, dv_acc)):
            flat_ref[:, which * width : (which + 1) * width] = acc[...].astype(BF16)


def self_backward(starts, query, key, value, out, grad, lse, block):
    tokens, width = query.shape
    heads = width // HEAD_DIM
    pieces = starts.shape[1]
    whole = pl.BlockSpec((tokens, width), lambda i, s: (0, 0))
    rows = pl.BlockSpec((block, width), lambda i, s: (i, 0))
    flops = 5 * 2 * heads * tokens * tokens * HEAD_DIM
    return pl.pallas_call(
        functools.partial(self_bwd_kernel, heads, pieces, block),
        out_shape=jax.ShapeDtypeStruct((tokens, 3 * width), BF16),
        grid_spec=pltpu.PrefetchScalarGridSpec(
            num_scalar_prefetch=1,
            grid=(tokens // block,),
            in_specs=[
                rows,
                whole,
                whole,
                rows,
                rows,
                pl.BlockSpec((heads, 8, block), lambda i, s: (0, 0, i)),
            ],
            out_specs=pl.BlockSpec((tokens, 3 * width), lambda i, s: (0, 0)),
            scratch_shapes=[pltpu.VMEM((tokens, width), F32), pltpu.VMEM((tokens, width), F32)],
        ),
        compiler_params=pltpu.CompilerParams(
            dimension_semantics=("arbitrary",), vmem_limit_bytes=VMEM_LIMIT
        ),
        cost_estimate=pl.CostEstimate(
            flops=flops, bytes_accessed=16 * tokens * width, transcendentals=heads * tokens * tokens
        ),
        name="self_backward",
    )(starts, query, key, value, out, grad, lse)


def cross_fwd_kernel(q_ref, k_ref, v_ref, o_ref, lse_ref):
    rows = q_ref.shape[0]
    for head in range(q_ref.shape[1] // HEAD_DIM):
        cols = slice(head * HEAD_DIM, (head + 1) * HEAD_DIM)
        scores = dot_nt(q_ref[:, cols] * BF16(SCALE), k_ref[:, cols])
        peak = jnp.max(scores, axis=1, keepdims=True)
        terms = jnp.exp(scores - peak)
        total = jnp.sum(terms, axis=1, keepdims=True)
        o_ref[:, cols] = (dot_f32(terms.astype(BF16), v_ref[:, cols]) / total).astype(BF16)
        lse = jnp.broadcast_to(peak + jnp.log(total), (rows, 128))
        lse_ref[head] = jnp.transpose(lse)[:8]


def cross_forward(query, key_value):
    rows, width = query.shape
    keys = key_value.shape[1]
    heads = width // HEAD_DIM
    return pl.pallas_call(
        lambda q, k, v, o, lse: cross_fwd_kernel(q, k, v, o, lse),
        out_shape=(
            jax.ShapeDtypeStruct((rows, width), BF16),
            jax.ShapeDtypeStruct((heads, 8, rows), F32),
        ),
        grid=(width // 128,),
        in_specs=[
            pl.BlockSpec((rows, 128), lambda i: (0, i)),
            pl.BlockSpec((None, keys, 128), lambda i: (0, 0, i)),
            pl.BlockSpec((None, keys, 128), lambda i: (1, 0, i)),
        ],
        out_specs=(
            pl.BlockSpec((rows, 128), lambda i: (0, i)),
            pl.BlockSpec((2, 8, rows), lambda i: (i, 0, 0)),
        ),
        compiler_params=pltpu.CompilerParams(
            dimension_semantics=("arbitrary",), vmem_limit_bytes=VMEM_LIMIT
        ),
        cost_estimate=pl.CostEstimate(
            flops=4 * rows * keys * width,
            bytes_accessed=4 * rows * width + 4 * keys * width,
            transcendentals=heads * rows * keys,
        ),
        name="cross_forward",
    )(query, key_value, key_value)


def cross_bwd_kernel(width, q_ref, k_ref, v_ref, o_ref, do_ref, lse_ref, dq_ref, dkv_ref):
    for head in range(q_ref.shape[1] // HEAD_DIM):
        cols = slice(head * HEAD_DIM, (head + 1) * HEAD_DIM)
        owner = head * HEAD_DIM // width
        own_cols = slice(head * HEAD_DIM % width, head * HEAD_DIM % width + HEAD_DIM)
        query = q_ref[:, cols] * BF16(SCALE)
        grad = do_ref[:, cols]
        product = grad.astype(F32) * o_ref[:, cols].astype(F32)
        delta = lax.dot_general(
            jnp.ones((8, HEAD_DIM), F32),
            product,
            NT,
            precision=lax.Precision.HIGHEST,
            preferred_element_type=F32,
        )[:1]
        key = k_ref[:, cols]
        weights = jnp.exp(dot_nt(key, query) - lse_ref[head][:1])
        grad_weights = dot_nt(v_ref[:, cols], grad)
        dkv_ref[owner, 1, :, own_cols] = dot_f32(weights.astype(BF16), grad).astype(BF16)
        grad_scores = (weights * (grad_weights - delta)).astype(BF16)
        dkv_ref[owner, 0, :, own_cols] = dot_f32(grad_scores, query).astype(BF16)
        dq_ref[:, cols] = (dot_tn(grad_scores, key) * SCALE).astype(BF16)


def cross_backward(query, key_value, out, grad, lse, owner_width):
    rows, width = query.shape
    keys = key_value.shape[1]
    heads = width // HEAD_DIM
    rows_spec = pl.BlockSpec((rows, 128), lambda i: (0, i))
    dkv_block = (128 // owner_width, 2, keys, owner_width)
    return pl.pallas_call(
        functools.partial(cross_bwd_kernel, owner_width),
        out_shape=(
            jax.ShapeDtypeStruct((rows, width), BF16),
            jax.ShapeDtypeStruct((width // owner_width, 2, keys, owner_width), BF16),
        ),
        grid=(width // 128,),
        in_specs=[
            rows_spec,
            pl.BlockSpec((None, keys, 128), lambda i: (0, 0, i)),
            pl.BlockSpec((None, keys, 128), lambda i: (1, 0, i)),
            rows_spec,
            rows_spec,
            pl.BlockSpec((2, 8, rows), lambda i: (i, 0, 0)),
        ],
        out_specs=(rows_spec, pl.BlockSpec(dkv_block, lambda i: (i, 0, 0, 0))),
        compiler_params=pltpu.CompilerParams(
            dimension_semantics=("arbitrary",), vmem_limit_bytes=VMEM_LIMIT
        ),
        cost_estimate=pl.CostEstimate(
            flops=10 * rows * keys * width,
            bytes_accessed=8 * rows * width + 8 * keys * width,
            transcendentals=heads * rows * keys,
        ),
        name="cross_backward",
    )(query, key_value, key_value, out, grad, lse)


def swap(values, axis, offset):
    count = lax.axis_size(axis)
    return lax.ppermute(values, axis, [(index, index ^ offset) for index in range(count)])


def dp_gather(values):
    return [values] + [swap(values, "dp", k) for k in range(1, lax.axis_size("dp"))]


def swap_blocks(blocks, axis):
    return [blocks[0]] + [swap(blocks[k], axis, k) for k in range(1, len(blocks))]


def pick_blocks(values, axis_name, axis):
    index = lax.axis_index(axis_name)
    return [
        lax.dynamic_index_in_dim(values, index ^ k, axis, keepdims=False)
        for k in range(values.shape[axis])
    ]


def tree_sum(parts):
    parts = [part.astype(F32) for part in parts]
    while len(parts) > 1:
        parts = [parts[k] + parts[k + 1] for k in range(0, len(parts), 2)]
    return parts[0]


def sum_along(values, axis):
    count = lax.axis_size(axis)
    return tree_sum([values] + [swap(values, axis, k) for k in range(1, count)])


def position():
    return jnp.stack([lax.axis_index(axis) for axis in ("dp",) + SEQ]).astype(jnp.int32)


def place_kernel(store, at_ref, *refs):
    store(at_ref[0], at_ref[1], at_ref[2], refs[:-1], refs[-1])


def place(parts, store, shape, block=None, part_blocks=None):
    steps = 1 if block is None else shape[0]
    block = shape if block is None else block
    part_blocks = [part.shape for part in parts] if part_blocks is None else part_blocks

    def spec(dims):
        return pl.BlockSpec(dims, lambda i, at: (i,) + (0,) * (len(dims) - 1))

    return pl.pallas_call(
        functools.partial(place_kernel, store),
        out_shape=jax.ShapeDtypeStruct(shape, parts[0].dtype),
        grid_spec=pltpu.PrefetchScalarGridSpec(
            num_scalar_prefetch=1,
            grid=(steps,),
            in_specs=[spec(dims) for dims in part_blocks],
            out_specs=spec(block),
        ),
        compiler_params=pltpu.CompilerParams(
            dimension_semantics=("arbitrary",), vmem_limit_bytes=VMEM_LIMIT
        ),
        cost_estimate=pl.CostEstimate(
            flops=0, bytes_accessed=4 * math.prod(shape), transcendentals=0
        ),
        name="place",
    )(position(), *parts)


def join_parts(parts, axis):
    shape = parts[0].shape
    full = shape[:axis] + (len(parts),) + shape[axis:]

    def store(dp_index, chip, core, refs, out):
        for k, ref in enumerate(refs):
            if axis == 0:
                out[dp_index ^ k] = ref[...]
            else:
                for lead in range(shape[0]):
                    where = (lead,) + (slice(None),) * (axis - 1) + (dp_index ^ k,)
                    out[where] = ref[lead]

    return place(parts, store, full)


def own_part(values, axis):
    return lax.dynamic_index_in_dim(values, lax.axis_index("dp"), axis, keepdims=False)


def fetch_columns(own):
    half = own.shape[1] // 2
    mine = lax.dynamic_slice_in_dim(own, lax.axis_index("core") * half, half, 1)
    return [swap(mine, "dp", k) for k in range(1, lax.axis_size("dp"))]


def share_columns(parts):
    return [swap(part, "core", 1) for part in parts]


def join_rows(parts):
    def store(dp_index, chip, core, refs, out):
        for k, ref in enumerate(refs):
            for flip in range(2):
                out[(chip ^ k) * 2 + (core ^ flip)] = ref[flip]

    return place(parts, store, (2 * len(parts),) + parts[0].shape[1:])


def join_fetched(parts):
    count, model, cut = parts[0].shape
    half = model // 2
    others = (len(parts) - 1) // 2

    def store(dp_index, chip, core, refs, out):
        out[0, :, pl.ds(pl.multiple_of(dp_index * cut, 128), cut)] = refs[0][0]
        for flip in range(2):
            rows = pl.ds(pl.multiple_of((core ^ flip) * half, 128), half)
            for k in range(1, others + 1):
                columns = pl.ds(pl.multiple_of((dp_index ^ k) * cut, 128), cut)
                out[0, rows, columns] = refs[flip * others + k][0]

    blocks = [(1,) + part.shape[1:] for part in parts]
    return place(parts, store, (count, model, model), (1, model, model), blocks)


def after(values, marker):
    return lax.optimization_barrier((values, marker))[0]


def meet(*values):
    return lax.optimization_barrier(values)


def take_columns_kernel(at_ref, in_ref, out_ref):
    out_ref[...] = in_ref[...].astype(BF16)


def take_columns(weights, shards, groups, cut):
    rows = weights.shape[0]
    if cut % 128:
        cut_up = own_part(weights.reshape(rows, shards, groups, cut), 2)
        return cut_up.reshape(rows, shards * cut).astype(BF16)
    return pl.pallas_call(
        take_columns_kernel,
        out_shape=jax.ShapeDtypeStruct((rows, shards * cut), BF16),
        grid_spec=pltpu.PrefetchScalarGridSpec(
            num_scalar_prefetch=1,
            grid=(shards,),
            in_specs=[pl.BlockSpec((rows, cut), lambda s, at: (0, s * groups + at[0]))],
            out_specs=pl.BlockSpec((rows, cut), lambda s, at: (0, s)),
        ),
        cost_estimate=pl.CostEstimate(
            flops=0, bytes_accessed=6 * rows * shards * cut, transcendentals=0
        ),
        name="take_columns",
    )(lax.axis_index("dp").astype(jnp.int32)[None], weights)


def encoder_partial_kernel(at_ref, grad_ref, key_ref, value_ref, out_ref):
    total = dot_nt(grad_ref[0], key_ref[...]) + dot_nt(grad_ref[1], value_ref[...])
    out_ref[...] = total.astype(BF16)


def encoder_partial(grad, w_keyed):
    rows, width = grad.shape[1:]
    model = w_keyed.shape[1]
    seq = lax.axis_index("chip") * lax.axis_size("core") + lax.axis_index("core")
    if width % 128:
        own = lax.dynamic_slice_in_dim(w_keyed, seq * width, width, 2)
        return (dot_nt(grad[0], own[0]) + dot_nt(grad[1], own[1])).astype(BF16)
    step = min(rows, 256)
    return pl.pallas_call(
        encoder_partial_kernel,
        out_shape=jax.ShapeDtypeStruct((rows, model), BF16),
        grid_spec=pltpu.PrefetchScalarGridSpec(
            num_scalar_prefetch=1,
            grid=(rows // step,),
            in_specs=[
                pl.BlockSpec((2, step, width), lambda i, at: (0, i, 0)),
                pl.BlockSpec((None, model, width), lambda i, at: (0, 0, at[0])),
                pl.BlockSpec((None, model, width), lambda i, at: (1, 0, at[0])),
            ],
            out_specs=pl.BlockSpec((step, model), lambda i, at: (i, 0)),
        ),
        compiler_params=pltpu.CompilerParams(
            dimension_semantics=("arbitrary",), vmem_limit_bytes=VMEM_LIMIT
        ),
        cost_estimate=pl.CostEstimate(
            flops=4 * rows * model * width, bytes_accessed=4 * rows * model, transcendentals=0
        ),
        name="encoder_partial",
    )(seq.astype(jnp.int32)[None], grad, w_keyed, w_keyed)


def join_natural_kernel(cut, in_ref, out_ref):
    groups = in_ref.shape[0]
    for index in range(groups):
        for s in range(in_ref.shape[2] // cut):
            start = (s * groups + index) * cut
            out_ref[:, start : start + cut] = in_ref[index, :, s * cut : (s + 1) * cut]


def join_natural(stacked, cut):
    groups, rows, columns = stacked.shape
    return pl.pallas_call(
        functools.partial(join_natural_kernel, cut),
        out_shape=jax.ShapeDtypeStruct((rows, columns * groups), stacked.dtype),
        compiler_params=pltpu.CompilerParams(vmem_limit_bytes=VMEM_LIMIT),
        cost_estimate=pl.CostEstimate(
            flops=0, bytes_accessed=4 * rows * columns * groups, transcendentals=0
        ),
        name="join_natural",
    )(stacked)


def dp_stack(values):
    copies = jnp.broadcast_to(values[None], (lax.axis_size("dp"),) + values.shape)
    return lax.all_to_all(copies, "dp", split_axis=0, concat_axis=0, tiled=True)


def clip_units(grad):
    mean_sq = jnp.mean(grad * grad, axis=-1, keepdims=True)
    return grad * jnp.minimum(1.0, CLIP_RMS * lax.rsqrt(mean_sq + CLIP_EPS))


def adam_update(weight, grad_sum, first_moment, second_moment):
    clipped = clip_units(grad_sum)
    first_new = BETA_ONE * first_moment + (1.0 - BETA_ONE) * clipped
    second_new = BETA_TWO * second_moment + (1.0 - BETA_TWO) * clipped * clipped
    step_size = first_new / CORRECT_ONE / (jnp.sqrt(second_new / CORRECT_TWO) + ADAM_EPS)
    return (first_new, second_new, -RATE * (step_size + DECAY * weight))


def adam_kernel(scale, g_ref, w_ref, m1_ref, m2_ref, g_out, m1_out, m2_out, change_out):
    grad = g_ref[...].astype(F32) * scale
    g_out[...] = grad
    m1_out[...], m2_out[...], change_out[...] = adam_update(
        w_ref[...], grad, m1_ref[...], m2_ref[...]
    )


def adam_call(grad, scale, weight, first, second):
    shape = weight.shape
    columns = shape[-1]
    rows = math.prod(shape[:-1])
    step = min(rows, 131072 // columns)
    spec = pl.BlockSpec((step, columns), lambda i: (i, 0))
    flat = jax.ShapeDtypeStruct((rows, columns), F32)
    outs = pl.pallas_call(
        functools.partial(adam_kernel, scale),
        out_shape=(flat,) * 4,
        grid=(rows // step,),
        in_specs=[spec] * 4,
        out_specs=(spec,) * 4,
        compiler_params=pltpu.CompilerParams(
            dimension_semantics=("arbitrary",), vmem_limit_bytes=VMEM_LIMIT
        ),
        cost_estimate=pl.CostEstimate(
            flops=20 * rows * columns, bytes_accessed=30 * rows * columns, transcendentals=0
        ),
        name="adam",
    )(*[array.reshape(rows, columns) for array in (grad, weight, first, second)])
    return [array.reshape(shape) for array in outs]


def gelu_both(values_in):
    root = math.sqrt(2.0 / math.pi)
    square = values_in * values_in
    bent = jnp.tanh(root * (values_in + 0.044715 * values_in * square))
    half = 0.5 * (1.0 + bent)
    slope = half + 0.5 * values_in * (1.0 - bent * bent) * root * (1.0 + 3.0 * 0.044715 * square)
    return values_in * half, slope.astype(BF16)


def on_device(
    hidden,
    encoder,
    piece_starts,
    grad_out,
    attn_in,
    attn_out,
    ffn_in,
    ffn_out,
    norms,
    first_attn_in,
    first_attn_out,
    first_ffn_in,
    first_ffn_out,
    first_norms,
    second_attn_in,
    second_attn_out,
    second_ffn_in,
    second_ffn_out,
    second_norms,
):
    groups = lax.axis_size("dp")
    shards = lax.axis_size("chip") * lax.axis_size("core")
    rows, model = hidden.shape
    tokens = rows * shards
    width = model // shards
    shard_rows = attn_in.shape[1]
    part_rows = shard_rows // groups
    hidden_units = ffn_in.shape[1]
    unit_cut = hidden_units // (shards * groups)
    block = min(512, tokens)

    core = lax.axis_index("core")
    chips = shards // 2
    gains = lax.optimization_barrier(norms.astype(BF16)).astype(F32)
    resid_in = hidden.astype(F32)
    normed_one, norm_one_back = jax.vjp(layer_norm, resid_in, gains[0], gains[1])
    normed_one = normed_one.astype(BF16)
    normed_all = lax.all_gather(normed_one, SEQ, axis=0, tiled=True)

    to_heads = own_part(attn_in[:3].reshape(3, groups, part_rows, shards, width), 1).astype(BF16)
    to_heads = to_heads.transpose(2, 1, 0, 3).reshape(shards, part_rows, 3 * width)
    to_heads = lax.all_to_all(to_heads, SEQ, split_axis=0, concat_axis=0, tiled=True)
    to_heads = dp_gather(to_heads)
    grad_parts = dp_gather(grad_out)

    def column_part(weights):
        cut = weights.reshape(weights.shape[0], shard_rows, groups, model // groups)
        return own_part(cut, 2).astype(BF16)

    enc_rows = encoder.shape[0]
    keyed = jnp.concatenate(
        [
            column_part(attn_in[4:]),
            encoder.reshape(enc_rows, groups, model // groups).transpose(1, 0, 2),
        ],
        axis=0,
    )
    outer = column_part(jnp.concatenate([attn_out[:1], attn_in[3:4], attn_out[1:]], axis=0))
    up = take_columns(ffn_in, shards, groups, unit_cut)
    down = own_part(ffn_out.reshape(groups, unit_cut, model), 0).astype(BF16)
    to_heads = join_parts(to_heads, 1).reshape(model, 3 * width)
    grad_tokens = jnp.concatenate(grad_parts, axis=0)
    normed_all, to_heads, grad_tokens, keyed, outer, up, down = meet(
        normed_all, to_heads, grad_tokens, keyed, outer, up, down
    )

    outer = lax.all_gather(outer, SEQ, axis=1, tiled=True)
    qkv = dot_f32(normed_all, to_heads).astype(BF16)
    keyed = lax.all_gather(after(keyed, qkv), SEQ, axis=1, tiled=True)
    query, key, value = [qkv[:, i * width : (i + 1) * width] for i in range(3)]
    out_heads, self_lse = self_forward(piece_starts, query, key, value, block)
    w_up = lax.all_gather(after(up, out_heads), SEQ, axis=0, tiled=True)
    attended = lax.all_to_all(
        out_heads.reshape(shards, rows, width), SEQ, split_axis=0, concat_axis=0, tiled=True
    )
    outer = after(outer, out_heads)
    outer_parts = fetch_columns(outer[:2])
    attended, outer_parts = meet(attended, outer_parts)
    w_down = lax.all_gather(after(down, attended), SEQ, axis=0, tiled=True)
    outer_shared = share_columns(outer_parts)
    w_o, w_cq = join_fetched([outer[:2]] + outer_parts + outer_shared)
    attended = attended.transpose(1, 0, 2).reshape(rows, model)
    first_sum = resid_in + dot_f32(attended, w_o)
    first_sum, keyed = meet(first_sum, keyed)

    keyed_parts = fetch_columns(keyed[:2])
    normed_two, norm_two_back = jax.vjp(layer_norm, first_sum, gains[2], gains[3])
    normed_two = normed_two.astype(BF16)
    cross_queries = dot_f32(normed_two, w_cq).astype(BF16)
    encoder_all = keyed[2:].transpose(1, 0, 2).reshape(enc_rows * shards, model)
    cross_queries, encoder_all, keyed_parts = meet(cross_queries, encoder_all, keyed_parts)
    w_keyed = join_fetched([keyed[:2]] + keyed_parts + share_columns(keyed_parts))
    cross_kv = jnp.stack([dot_f32(encoder_all, w_keyed[i]) for i in range(2)]).astype(BF16)

    cross_parts = fetch_columns(after(outer[2:], cross_kv))
    crossed, cross_lse = cross_forward(cross_queries, cross_kv)
    crossed, cross_parts = meet(crossed, cross_parts)
    w_co = join_fetched([outer[2:]] + cross_parts + share_columns(cross_parts))[0]
    second_sum = first_sum + dot_f32(crossed, w_co)

    normed_three, norm_three_back = jax.vjp(layer_norm, second_sum, gains[4], gains[5])
    normed_three = normed_three.astype(BF16)
    ffn_tokens = jnp.concatenate(dp_gather(normed_three), axis=0)
    activated, slope = gelu_both(dot_f32(ffn_tokens, w_up))
    activated = activated.astype(BF16)
    grad_down = dot_tn(activated, grad_tokens).astype(BF16)
    activated, slope = after((activated, slope), grad_down)
    grad_down = lax.psum_scatter(grad_down, SEQ, scatter_dimension=0, tiled=True)
    grad_pre = (dot_nt(grad_tokens, w_down) * slope).astype(BF16)
    partial = dot_nt(grad_pre, w_up).astype(BF16)
    grad_three = swap_blocks([partial[k * rows : (k + 1) * rows] for k in range(groups)], "dp")

    activated, grad_pre = after((activated, grad_pre), partial)
    partial = dot_f32(activated, w_down)
    grad_up = dot_tn(ffn_tokens, grad_pre).astype(BF16)
    grad_three, layer_out, grad_up = meet(grad_three, partial.astype(BF16), grad_up)
    grad_up = lax.psum_scatter(grad_up, SEQ, scatter_dimension=0, tiled=True)
    norm_part, grad_gain_three, grad_shift_three = norm_three_back(tree_sum(grad_three))
    grad_second = grad_out.astype(F32) + norm_part
    grad_cross_branch = grad_second.astype(BF16)
    grad_cross_branch, grad_down = meet(grad_cross_branch, grad_down)
    down_parts = dp_gather(grad_down)
    grad_crossed = dot_nt(grad_cross_branch, w_co).astype(BF16)
    grad_cq, grad_ckv = cross_backward(
        cross_queries, cross_kv, crossed, grad_crossed, cross_lse, width
    )
    grad_cq, down_parts, grad_ckv, layer_out = meet(grad_cq, down_parts, grad_ckv, layer_out)
    hidden_parts = [layer_out[k * rows : (k + 1) * rows] for k in range(groups)]
    early_parts = swap_blocks(hidden_parts[:3], "dp")
    grad_ckv = lax.psum_scatter(grad_ckv, SEQ, scatter_dimension=0, tiled=True)
    grad_ckv = grad_ckv.reshape(2, enc_rows * shards, width)
    grad_normed_two = dot_nt(grad_cq, w_cq)
    norm_part, grad_gain_two, grad_shift_two = norm_two_back(grad_normed_two)
    grad_first = grad_second + norm_part
    grad_self_branch = grad_first.astype(BF16)
    grad_attended = dot_nt(grad_self_branch, w_o).astype(BF16)
    grad_w_co = dot_tn(crossed, grad_cross_branch)
    grad_w_cq = dot_tn(normed_two, grad_cq)
    grad_w_o = dot_tn(attended, grad_self_branch)
    local = jnp.stack([grad.astype(BF16) for grad in (grad_w_o, grad_w_co, grad_w_cq)])
    local = pick_blocks(local.reshape(3, chips, 2, shard_rows, model), "core", 2)
    grad_attended, local, early_parts = meet(grad_attended, local, early_parts)
    grad_heads = lax.all_to_all(
        grad_attended.reshape(rows, shards, width).transpose(1, 0, 2),
        SEQ,
        split_axis=0,
        concat_axis=0,
        tiled=True,
    ).reshape(tokens, width)

    scale = 1.0 / math.sqrt(tokens * groups)
    local = swap_blocks(local, "core")
    whole_down = join_parts(after(down_parts, grad_attended), 0)
    local, whole_down = meet(local, whole_down)
    local = tree_sum(local).astype(BF16).reshape(3, chips, groups, part_rows, model)
    local = pick_blocks(local, "dp", 2)
    local, whole_down = meet(local, whole_down)
    local = swap_blocks(local, "dp")
    sum_down, *upd_down = adam_call(whole_down, scale, ffn_out, first_ffn_out, second_ffn_out)
    grad_heads, local[1], sum_down, grad_up = meet(grad_heads, local[1], sum_down, grad_up)

    grad_flat = self_backward(
        piece_starts, query, key, value, out_heads, grad_heads, self_lse, block
    )
    grad_flat, local = meet(grad_flat, local)

    def reduce_headed(inputs, grads):
        headed = dot_tn(inputs, grads).astype(BF16)
        return headed.reshape(shards, groups, part_rows, grads.shape[1])

    def headed_rows(headed):
        count = headed[0].shape[2] // width
        headed = join_rows(headed).reshape(shards, part_rows, count, width)
        return headed.transpose(2, 1, 0, 3).reshape(count, part_rows, model)

    partial = dot_nt(grad_flat, to_heads).astype(BF16)
    grad_normed_one = lax.psum_scatter(partial, SEQ, scatter_dimension=0, tiled=True)

    grad_flat, local, grad_up, hidden_parts = after((grad_flat, local, grad_up, hidden_parts), partial)
    late_parts = [swap(hidden_parts[k], "dp", k) for k in range(3, groups)]
    self_part = reduce_headed(normed_all, grad_flat)
    local = pick_blocks(tree_sum(local).astype(BF16), "chip", 1)
    grad_ckv, local, self_part, late_parts = meet(grad_ckv, local, self_part, late_parts)
    cross_part = reduce_headed(encoder_all, jnp.concatenate([grad_ckv[0], grad_ckv[1]], axis=1))
    headed = jnp.concatenate([self_part, cross_part], axis=3).transpose(1, 0, 2, 3)
    headed = lax.all_to_all(headed, "dp", split_axis=0, concat_axis=0, tiled=True)
    local = swap_blocks(local, "chip")
    partial_enc = encoder_partial(grad_ckv, w_keyed)
    out_hidden = second_sum + tree_sum(early_parts + late_parts)
    headed, partial_enc, local[:3], out_hidden = meet(headed, partial_enc, local[:3], out_hidden)

    whole_up = dp_stack(after(grad_up, headed))
    headed = jnp.sum(headed.astype(F32), axis=0).astype(BF16)
    own, given = pick_blocks(headed.reshape(chips, 2, part_rows, 5 * width), "core", 1)
    given = swap(given, "core", 1)
    given, own = meet(given, own)
    headed = pick_blocks(jnp.stack([own, given], axis=1), "chip", 0)
    headed = swap_blocks(headed, "chip")
    headed, local, whole_up, partial_enc = meet(headed, local, whole_up, partial_enc)
    grad_encoder = lax.psum_scatter(partial_enc, SEQ, scatter_dimension=0, tiled=True)
    local = tree_sum(local).astype(BF16)
    headed = headed_rows(headed)
    attn_parts = jnp.concatenate([headed[:3], local[2:], headed[3:], local[:2]])
    attn_parts = dp_gather(attn_parts)
    if unit_cut % 128:
        whole_up = whole_up.reshape(groups, shard_rows, shards, unit_cut).transpose(1, 2, 0, 3)
        whole_up = whole_up.reshape(shard_rows, hidden_units)
    else:
        whole_up = join_natural(whole_up, unit_cut)
    sum_up, *upd_up = adam_call(whole_up, scale, ffn_in, first_ffn_in, second_ffn_in)
    grad_normed_one, attn_parts, sum_up = meet(grad_normed_one, attn_parts, sum_up)
    norm_part, grad_gain_one, grad_shift_one = norm_one_back(grad_normed_one.astype(F32))
    grad_hidden = grad_first + norm_part
    sum_norms = jnp.stack(
        [
            grad_gain_one,
            grad_shift_one,
            grad_gain_two,
            grad_shift_two,
            grad_gain_three,
            grad_shift_three,
        ]
    )
    sum_norms = sum_along(sum_norms * scale, "core")
    whole_attn = join_parts(attn_parts, 1).reshape(8, shard_rows, model)
    sum_norms, whole_attn = meet(sum_norms, whole_attn)
    sum_norms = sum_along(sum_norms, "chip")
    sum_in, *upd_in = adam_call(whole_attn[:6], scale, attn_in, first_attn_in, second_attn_in)
    sum_norms, sum_in, grad_encoder = meet(sum_norms, sum_in, grad_encoder)
    norm_total = sum_along(sum_norms, "dp")
    sum_out, *upd_out = adam_call(whole_attn[6:], scale, attn_out, first_attn_out, second_attn_out)
    norm_total, sum_out = meet(norm_total, sum_out)
    grad_encoder = grad_encoder.astype(F32)
    upd_norms = adam_update(norms, norm_total, first_norms, second_norms)
    return (
        out_hidden,
        grad_hidden,
        grad_encoder,
        sum_in,
        sum_out,
        sum_up,
        sum_down,
        norm_total,
        upd_in[0],
        upd_out[0],
        upd_up[0],
        upd_down[0],
        upd_norms[0],
        upd_in[1],
        upd_out[1],
        upd_up[1],
        upd_down[1],
        upd_norms[1],
        upd_in[2],
        upd_out[2],
        upd_up[2],
        upd_down[2],
        upd_norms[2],
    )


def solution(mesh):
    groups, shards = mesh.shape["dp"], mesh.shape["seq"]
    split = Mesh(mesh.devices.reshape(groups, shards // 2, 2), ("dp",) + SEQ)
    token = P(("dp",) + SEQ, None)
    stacked = P(None, SEQ, None)
    flat = P(SEQ, None)
    params = (stacked, stacked, flat, flat, P())
    return jax.shard_map(
        on_device,
        mesh=split,
        in_specs=(token, token, P("dp", None), token) + params * 3,
        out_specs=(token, token, token) + params * 4,
        check_vma=False,
    )
```
